128 devices in a mesh: clip: 8 (over y, core), seq: 16 (over z, x).
Axes of the slice: x: 4, y: 4, z: 4, core: 2. Of those that a mesh axis runs over, the one named last changes fastest.
Arguments:
- query_raw: bfloat16 [8, 2048, 4096], P('clip', 'seq'), may hold values from -16 to 16
- key_raw: bfloat16 [8, 2048, 4096], P('clip', 'seq'), may hold values from -16 to 16
- value: bfloat16 [8, 2048, 4096], P('clip', 'seq'), may hold values from -6 to 6
- upstream: bfloat16 [8, 2048, 4096], P('clip', 'seq'), may hold values from -6 to 6
- query_gain: float32 [4096], replicated, may hold values from 0.5 to 1.5
- key_gain: float32 [4096], replicated, may hold values from 0.5 to 1.5
- key_blocks: int32 [8, 32, 16, 4], P('clip'), may hold values from 0 to 15, as said below
- live: int32 [8, 32], P('clip'), may hold values from 2 to 4, as said below
Outputs:
- attended: bfloat16 [8, 2048, 4096], P('clip', 'seq')
- grad_query: bfloat16 [8, 2048, 4096], P('clip', 'seq')
- grad_key: bfloat16 [8, 2048, 4096], P('clip', 'seq')
- grad_value: bfloat16 [8, 2048, 4096], P('clip', 'seq')
- grad_query_gain: float32 [4096], replicated
- grad_key_gain: float32 [4096], replicated
The draws below stay inside these ranges and needn't reach their ends.
Inputs may be any that keep to these rules, and one draw needn't show every extreme that they name: key_blocks[c, h, b, 0] equals b, and the 4 entries of one row are distinct. Only the first live[c, h] entries of a row are selected. `live`: in every clip at least one head uses all 4 entries.
All inputs are finite; a program needn't handle non-finite values.
Results may differ from the reference program's by a relative error of at most 0.035.
Values may be sent and summed in bfloat16 or wider, within the bound.
No kernel may reach another device: no remote copies, remote signals or barrier semaphores. Data moves between devices by JAX's collectives and lax.ppermute only.
A program may use at most 128 MiB of HBM per device.

```python
import jax
import jax.numpy as jnp
from jax import lax

H = 32
HD = 128
BLK = 128
SELMAX = 4
CLIPS = 8
LEN = 2048
QB = 16
D_ATT = 4096


def feature_field(key, salt):
    base_key = jax.random.fold_in(key, salt)
    return jnp.clip(jax.random.normal(base_key, (CLIPS, LEN, D_ATT), jnp.float32), -6.0, 6.0)


def draw_query_raw(key, part):
    field = feature_field(key, 601)
    return field.astype(jnp.bfloat16)


def draw_key_raw(key, part):
    field = feature_field(key, 701)
    return field.astype(jnp.bfloat16)


def draw_key_blocks(key, part):
    base_key = jax.random.fold_in(key, 801)
    others = QB - 1
    rank_keys = jax.random.randint(base_key, (CLIPS, H, QB, others), 0, 1 << 20) * others + jnp.arange(others, dtype=jnp.int32)
    picked = jnp.argsort(rank_keys, axis=-1, stable=True)[..., :SELMAX - 1].astype(jnp.int32) + 1
    own_block = jnp.arange(QB, dtype=jnp.int32)[None, None, :, None]
    chosen = (own_block + picked) % QB
    return jnp.concatenate([jnp.broadcast_to(own_block, (CLIPS, H, QB, 1)), chosen], axis=-1).astype(jnp.int32)


def draw_live(key, part):
    base_key = jax.random.fold_in(key, 901)
    key_one, key_two, key_three = jax.random.split(base_key, 3)
    lower = jax.random.randint(key_one, (CLIPS, H), 0, SELMAX - 1)
    upper = jax.random.randint(key_two, (CLIPS, H), 0, SELMAX - 1)
    heavy = jax.random.randint(key_three, (CLIPS, 1), 0, H)
    counts = 2 + jnp.minimum(lower, upper)
    return jnp.where(jnp.arange(H)[None, :] == heavy, SELMAX, counts).astype(jnp.int32)


def level_of(rng, extent, cuts, least, high):
    loudness = 1.0
    for position, blocks in cuts:
        draws = jax.random.uniform(jax.random.fold_in(jax.random.fold_in(rng, 6), position), (blocks,), jnp.float32, least / len(cuts), high / len(cuts))
        loudness = loudness * jnp.repeat(jnp.exp(draws), extent[position] // blocks).reshape((-1,) + (1,) * (len(extent) - 1 - position))
    return loudness


def bell_draw(rng, extent, spread, limit, cuts=(), kind=jnp.bfloat16):
    drawn = spread * jax.random.normal(rng, extent, jnp.float32)
    if cuts:
        drawn = drawn * level_of(rng, extent, cuts, -0.22, 0.18)
    return jnp.clip(drawn, -limit, limit).astype(kind)


def setup_inputs(seed: int = 0) -> dict:
    seeds = jax.random.split(jax.random.key(seed), 9)
    return {
        "query_raw": draw_query_raw(jax.random.fold_in(seeds[8], 71), 0),
        "key_raw": draw_key_raw(jax.random.fold_in(seeds[8], 71), 0),
        "value": bell_draw(seeds[2], (CLIPS, LEN, D_ATT), 1.0, 6.0, ((0, 8), (1, 16))),
        "upstream": bell_draw(seeds[3], (CLIPS, LEN, D_ATT), 1.0, 6.0, ((0, 8), (1, 16))),
        "query_gain": jnp.clip(1.0 + 0.1 * jax.random.normal(seeds[4], (D_ATT,), jnp.float32), 0.5, 1.5),
        "key_gain": jnp.clip(1.0 + 0.1 * jax.random.normal(seeds[5], (D_ATT,), jnp.float32), 0.5, 1.5),
        "key_blocks": draw_key_blocks(jax.random.fold_in(seeds[8], 71), 0),
        "live": draw_live(jax.random.fold_in(seeds[8], 71), 0),
    }


EPSILON = 1e-06
blocks_per_step = 4

def norm_forward(raw, gain):
    values = raw.astype(jnp.float32)
    inverse = lax.rsqrt(lax.optimization_barrier(jnp.mean(values * values, axis=-1, keepdims=True)) + EPSILON)
    unit_rows = values * inverse
    return (unit_rows, inverse, (unit_rows * gain).astype(jnp.bfloat16))

def norm_backward(unit_rows, inverse, gain, upstream):
    incoming = upstream.astype(jnp.float32)
    scaled = incoming * gain
    inner_mean = lax.optimization_barrier(jnp.mean(scaled * unit_rows, axis=-1, keepdims=True))
    unscaled_gradient = (inverse * (scaled - unit_rows * inner_mean)).astype(jnp.bfloat16)
    grad_gain = lax.optimization_barrier(jnp.sum((incoming * unit_rows).reshape(-1, unit_rows.shape[-1]), axis=0))
    return (unscaled_gradient, grad_gain)

def round_back(array):
    return lax.optimization_barrier(array.astype(jnp.bfloat16)).astype(jnp.float32)

def head_pass(queries, key_rows, values, upstream, block_lists, used_count):
    length, head_width = queries.shape
    block_count = length // BLK
    score_scale = head_width ** (-0.5)
    q_blocks = queries.reshape(block_count, BLK, head_width).astype(jnp.float32)
    k_blocks = key_rows.reshape(block_count, BLK, head_width).astype(jnp.float32)
    v_blocks = values.reshape(block_count, BLK, head_width).astype(jnp.float32)
    u_blocks = upstream.reshape(block_count, BLK, head_width).astype(jnp.float32)
    selected = jnp.arange(block_lists.shape[1], dtype=jnp.int32) < used_count

    def group_step(carry, index):
        grad_keys, grad_values = carry
        first_block = (index * blocks_per_step).astype(jnp.int32)
        row_lists = lax.dynamic_slice_in_dim(block_lists, first_block, blocks_per_step, 0)
        q_four = lax.dynamic_slice_in_dim(q_blocks, first_block, blocks_per_step, 0)
        u_four = lax.dynamic_slice_in_dim(u_blocks, first_block, blocks_per_step, 0)
        k_chosen = k_blocks[row_lists]
        v_chosen = v_blocks[row_lists]
        scores = jnp.einsum('gqd,gskd->gqsk', q_four, k_chosen) * score_scale
        scores = jnp.where(selected[None, None, :, None], scores, -jnp.inf)
        row_max = lax.optimization_barrier(jnp.max(scores, axis=(2, 3), keepdims=True))
        raised = jnp.exp(scores - row_max)
        weights = raised / lax.optimization_barrier(jnp.sum(raised, axis=(2, 3), keepdims=True))
        weights_low = round_back(weights)
        attended = jnp.einsum('gqsk,gskd->gqd', weights_low, v_chosen).astype(jnp.bfloat16)
        attended_wide = lax.optimization_barrier(attended).astype(jnp.float32)
        delta = lax.optimization_barrier(jnp.sum(u_four * attended_wide, axis=-1))
        grad_weights = jnp.einsum('gqd,gskd->gqsk', u_four, v_chosen)
        grad_low = round_back(weights * (grad_weights - delta[:, :, None, None]) * score_scale)
        grad_query = jnp.einsum('gqsk,gskd->gqd', grad_low, k_chosen).astype(jnp.bfloat16)
        grad_keys = grad_keys.at[row_lists].add(jnp.einsum('gqsk,gqd->gskd', grad_low, q_four))
        grad_values = grad_values.at[row_lists].add(jnp.einsum('gqsk,gqd->gskd', weights_low, u_four))
        return ((grad_keys, grad_values), (attended, grad_query))
    empty_grad = jnp.zeros((block_count, BLK, head_width), jnp.float32)
    step_index = jnp.arange(block_count // blocks_per_step, dtype=jnp.int32)
    (grad_keys, grad_values), (attended, grad_query) = lax.scan(group_step, (empty_grad, empty_grad), step_index)
    return (attended.reshape(length, head_width), grad_query.reshape(length, head_width), grad_keys.reshape(length, head_width).astype(jnp.bfloat16), grad_values.reshape(length, head_width).astype(jnp.bfloat16))

def split_heads(array):
    return array.reshape(array.shape[0], H, HD).transpose(1, 0, 2)

def merge_heads(array):
    return array.transpose(1, 0, 2).reshape(array.shape[1], H * HD)

def clip_sweep(inputs):
    q_clip, k_clip, v_clip, u_clip, list_clip, live_clip = inputs

    def one_head(head_inputs):
        q_head, k_head, v_head, u_head, list_head, live_head = head_inputs
        return head_pass(q_head, k_head, v_head, u_head, list_head, live_head)
    results = lax.map(one_head, (split_heads(q_clip), split_heads(k_clip), split_heads(v_clip), split_heads(u_clip), list_clip, live_clip))
    return tuple((merge_heads(member) for member in results))

def reference(query_raw, key_raw, value, upstream, query_gain, key_gain, key_blocks, live):
    q_unit, q_inverse, q_normed = norm_forward(query_raw, query_gain)
    k_unit, k_inverse, k_normed = norm_forward(key_raw, key_gain)
    attended, grad_q_normed, grad_k_normed, grad_value = lax.map(clip_sweep, (q_normed, k_normed, value, upstream, key_blocks, live))
    grad_query, grad_query_gain = norm_backward(q_unit, q_inverse, query_gain, grad_q_normed)
    grad_key, grad_key_gain = norm_backward(k_unit, k_inverse, key_gain, grad_k_normed)
    return (attended, grad_query, grad_key, grad_value, grad_query_gain, grad_key_gain)
```

```python
import jax
import jax.numpy as jnp
from jax import lax
from jax.experimental import pallas as pl
from jax.experimental.pallas import tpu as pltpu
from jax.sharding import PartitionSpec as P

BLK = 128
EPSILON = 1e-06
ROWS = 16
QUERY, KEY, VALUE, COTANGENT = range(4)
OUT, GRAD_Q, GRAD_K, GRAD_V = range(4)
LOG2E = 1.4426950408889634


def contract(a, b, dims):
    return lax.dot_general(a, b, (dims, ((), ())), preferred_element_type=jnp.float32)


def inverse_rms(x):
    return lax.rsqrt(jnp.mean(x * x, axis=-1, keepdims=True) + EPSILON)


def pack_kernel(q_ref, k_ref, v_ref, u_ref, qg_ref, kg_ref, out_ref):
    groups, _, heads, _, width = out_ref.shape

    def put(kind, rows):
        for group in range(groups):
            for head in range(heads):
                at = (group * heads + head) * width
                out_ref[group, kind, head] = rows[:, at : at + width]

    for kind, ref, gain_ref in ((QUERY, q_ref, qg_ref), (KEY, k_ref, kg_ref)):
        x = ref[...].astype(jnp.float32)
        put(kind, (x * inverse_rms(x) * gain_ref[...]).astype(jnp.bfloat16))
    put(VALUE, v_ref[...])
    put(COTANGENT, u_ref[...])


def pack(q, k, v, u, q_gain, k_gain, groups, heads):
    tokens, features = q.shape
    width = features // (groups * heads)
    rows = pl.BlockSpec((ROWS, features), lambda i: (i, 0))
    gain = pl.BlockSpec((1, features), lambda i: (0, 0))
    return pl.pallas_call(
        pack_kernel,
        grid=(tokens // ROWS,),
        in_specs=[rows] * 4 + [gain] * 2,
        out_specs=pl.BlockSpec((groups, 4, heads, ROWS, width), lambda i: (0, 0, 0, i, 0)),
        out_shape=jax.ShapeDtypeStruct((groups, 4, heads, tokens, width), jnp.bfloat16),
        name="pack",
    )(q, k, v, u, q_gain[None], k_gain[None])


def attention_kernel(lists_ref, live_ref, in_ref, out_ref, gains_ref, kt_ref, vt_ref, dk_ref, dv_ref):
    blocks, _, heads, _, width = in_ref.shape
    scale = width ** (-0.5)

    for head in range(heads):

        def prepare(j, carry):
            kt_ref[j] = in_ref[j, KEY, head].T
            vt_ref[j] = in_ref[j, VALUE, head].T
            dk_ref[j] = jnp.zeros((BLK, width), jnp.float32)
            dv_ref[j] = jnp.zeros((BLK, width), jnp.float32)
            return carry

        lax.fori_loop(0, blocks, prepare, 0)

        def one_block(b, slots):
            q = in_ref[b, QUERY, head]
            u = in_ref[b, COTANGENT, head]
            chosen = [lists_ref[head, b, s] for s in range(slots)]
            scores = [contract(in_ref[j, KEY, head], q, ((1,), (1,))) for j in chosen]
            grads = [contract(in_ref[j, VALUE, head], u, ((1,), (1,))) for j in chosen]
            top = scores[0]
            for s in scores[1:]:
                top = jnp.maximum(top, s)
            top = jnp.max(top, axis=0, keepdims=True) * (scale * LOG2E)
            raised = [jnp.exp2(s * (scale * LOG2E) - top) for s in scores]
            total = raised[0]
            for e in raised[1:]:
                total = total + e
            inverse = 1.0 / jnp.sum(total, axis=0, keepdims=True)
            probs = [e * inverse for e in raised]
            inner = probs[0] * grads[0]
            for p, g in zip(probs[1:], grads[1:]):
                inner = inner + p * g
            delta = jnp.sum(inner, axis=0, keepdims=True)
            low = [p.astype(jnp.bfloat16) for p in probs]
            ds = [(p * (g - delta) * scale).astype(jnp.bfloat16) for p, g in zip(probs, grads)]
            out_t = contract(vt_ref[chosen[0]], low[0], ((1,), (0,)))
            dq_t = contract(kt_ref[chosen[0]], ds[0], ((1,), (0,)))
            for j, p, d in zip(chosen[1:], low[1:], ds[1:]):
                out_t = out_t + contract(vt_ref[j], p, ((1,), (0,)))
                dq_t = dq_t + contract(kt_ref[j], d, ((1,), (0,)))
            out_ref[b, OUT, head] = out_t.T.astype(jnp.bfloat16)
            dq = dq_t.T.astype(jnp.bfloat16)
            out_ref[b, GRAD_Q, head] = dq
            for j, p, d in zip(chosen, low, ds):
                dv_ref[j] += contract(p, u, ((1,), (0,)))
                dk_ref[j] += contract(d, q, ((1,), (0,)))
            return jnp.sum(dq.astype(jnp.float32) * q.astype(jnp.float32), axis=0, keepdims=True)

        gains_ref[head : head + 1] = jnp.zeros((1, width), jnp.float32)
        for slots in (2, 3, 4):

            @pl.when(live_ref[head] == slots)
            def _():
                def step(b, gain):
                    return gain + one_block(b, slots)

                gains_ref[head : head + 1] = lax.fori_loop(
                    0, blocks, step, jnp.zeros((1, width), jnp.float32)
                )

        def finish(j, gain):
            dk = dk_ref[j].astype(jnp.bfloat16)
            out_ref[j, GRAD_K, head] = dk
            out_ref[j, GRAD_V, head] = dv_ref[j].astype(jnp.bfloat16)
            k = in_ref[j, KEY, head].astype(jnp.float32)
            return gain + jnp.sum(dk.astype(jnp.float32) * k, axis=0, keepdims=True)

        gains_ref[heads + head : heads + head + 1] = lax.fori_loop(
            0, blocks, finish, jnp.zeros((1, width), jnp.float32)
        )


def attention(lists, live, arrived):
    blocks, _, heads, _, width = arrived.shape
    vmem = pl.BlockSpec(memory_space=pltpu.VMEM)
    smem = pl.BlockSpec(memory_space=pltpu.SMEM)
    return pl.pallas_call(
        attention_kernel,
        in_specs=[smem, smem, vmem],
        out_specs=[vmem, vmem],
        out_shape=[
            jax.ShapeDtypeStruct(arrived.shape, jnp.bfloat16),
            jax.ShapeDtypeStruct((2 * heads, width), jnp.float32),
        ],
        scratch_shapes=[
            pltpu.VMEM((blocks, width, BLK), jnp.bfloat16),
            pltpu.VMEM((blocks, width, BLK), jnp.bfloat16),
            pltpu.VMEM((blocks, BLK, width), jnp.float32),
            pltpu.VMEM((blocks, BLK, width), jnp.float32),
        ],
        name="attention",
    )(lists, live, arrived)


def unpack_kernel(back_ref, q_ref, k_ref, qg_ref, kg_ref, out_ref, dq_ref, dk_ref, dv_ref):
    groups, _, heads, _, width = back_ref.shape

    def take(kind):
        return jnp.concatenate(
            [back_ref[g, kind, h] for g in range(groups) for h in range(heads)], axis=-1
        )

    out_ref[...] = take(OUT)
    dv_ref[...] = take(GRAD_V)
    for kind, raw_ref, gain_ref, ref in (
        (GRAD_Q, q_ref, qg_ref, dq_ref),
        (GRAD_K, k_ref, kg_ref, dk_ref),
    ):
        x = raw_ref[...].astype(jnp.float32)
        inverse = inverse_rms(x)
        unit = x * inverse
        g = take(kind).astype(jnp.float32) * gain_ref[...]
        mean = jnp.mean(g * unit, axis=-1, keepdims=True)
        ref[...] = (inverse * (g - unit * mean)).astype(jnp.bfloat16)


def unpack(back, q, k, q_gain, k_gain):
    groups, _, heads, tokens, width = back.shape
    features = q.shape[1]
    rows = pl.BlockSpec((ROWS, features), lambda i: (i, 0))
    gain = pl.BlockSpec((1, features), lambda i: (0, 0))
    return pl.pallas_call(
        unpack_kernel,
        grid=(tokens // ROWS,),
        in_specs=[
            pl.BlockSpec((groups, 4, heads, ROWS, width), lambda i: (0, 0, 0, i, 0)),
            rows,
            rows,
            gain,
            gain,
        ],
        out_specs=[rows] * 4,
        out_shape=[jax.ShapeDtypeStruct((tokens, features), jnp.bfloat16)] * 4,
        name="unpack",
    )(back, q, k, q_gain[None], k_gain[None])


def exchange_sum(x, axis):
    size = lax.axis_size(axis)
    step = 1
    while step < size:
        x = x + lax.ppermute(x, axis, [(i, i ^ step) for i in range(size)])
        step *= 2
    return x


def shards(query_raw, key_raw, value, upstream, query_gain, key_gain, key_blocks, live):
    groups = lax.axis_size("seq")
    features = query_raw.shape[2]
    heads = key_blocks.shape[1] // groups
    mine = lax.axis_index("seq")
    lists = lax.dynamic_slice_in_dim(key_blocks[0], mine * heads, heads)
    counts = lax.dynamic_slice_in_dim(live[0], mine * heads, heads)
    packed = pack(
        query_raw[0], key_raw[0], value[0], upstream[0], query_gain, key_gain, groups, heads
    )
    arrived = lax.all_to_all(packed, "seq", split_axis=0, concat_axis=0, tiled=True)
    results, gains = attention(lists, counts, arrived)
    back = lax.all_to_all(results, "seq", split_axis=0, concat_axis=0, tiled=True)
    gains = exchange_sum(gains.reshape(1, -1), "clip")
    gains = jnp.where(jnp.arange(groups)[:, None] == mine, gains, 0.0)
    gains = exchange_sum(gains, "seq").reshape(groups, 2, -1)
    attended, grad_query, grad_key, grad_value = unpack(
        back, query_raw[0], key_raw[0], query_gain, key_gain
    )
    return (
        attended[None],
        grad_query[None],
        grad_key[None],
        grad_value[None],
        gains[:, 0].reshape(features) / query_gain,
        gains[:, 1].reshape(features) / key_gain,
    )


def solution(mesh):
    tokens = P("clip", "seq", None)
    return jax.shard_map(
        shards,
        mesh=mesh,
        in_specs=(tokens,) * 4 + (P(), P(), P("clip", None, None, None), P("clip", None)),
        out_specs=(tokens,) * 4 + (P(), P()),
        check_vma=False,
    )
```

```python
import jax
import jax.numpy as jnp
from jax import lax
from jax.experimental import pallas as pl
from jax.experimental.pallas import tpu as pltpu
from jax.sharding import PartitionSpec as P

BLK = 128
EPSILON = 1e-06
ROWS = 16
CHUNKS = 4
PARTS = 3
SPARE = 8
QUERY, COTANGENT, KEY, VALUE = range(4)
GRAD_Q, OUT, GRAD_K, GRAD_V = range(4)
LOG2E = 1.4426950408889634


def contract(a, b, dims):
    return lax.dot_general(a, b, (dims, ((), ())), preferred_element_type=jnp.float32)


def inverse_rms(x):
    return lax.rsqrt(jnp.mean(x * x, axis=-1, keepdims=True) + EPSILON)


def pack_kernel(
    q_hbm, k_hbm, v_hbm, u_hbm, qg_hbm, kg_hbm, out_ref, raw_ref, gain_ref, raw_sems, gain_sems, copy_sems
):
    groups, span, both = out_ref.shape
    width = both // 2
    tokens = raw_ref.shape[1]
    heads = span // (2 * tokens)
    step = tokens // CHUNKS

    loads = [
        [
            pltpu.make_async_copy(
                hbm.at[pl.ds(c * step, step)],
                raw_ref.at[n, pl.ds(c * step, step)],
                raw_sems.at[n, c],
            )
            for c in range(CHUNKS)
        ]
        for n, hbm in enumerate((q_hbm, k_hbm))
    ]
    gain_loads = [
        pltpu.make_async_copy(hbm, gain_ref.at[n], gain_sems.at[n])
        for n, hbm in enumerate((qg_hbm, kg_hbm))
    ]
    for n in range(2):
        gain_loads[n].start()
        loads[n][0].start()
    for c in range(1, CHUNKS):
        for n in range(2):
            loads[n][c].start()
    moves = []
    for group in range(groups):
        for head in range(heads):
            at = (group * heads + head) * width
            for n, (hbm, pair) in enumerate(((u_hbm, 0), (v_hbm, 1))):
                first = (pair * heads + head) * tokens
                moves.append(
                    pltpu.make_async_copy(
                        hbm.at[:, pl.ds(at, width)],
                        out_ref.at[group, pl.ds(first, tokens), pl.ds(width, width)],
                        copy_sems.at[group * heads + head, n],
                    )
                )
    for move in moves:
        move.start()
    for c in range(CHUNKS):
        for n in range(2):
            if c == 0:
                gain_loads[n].wait()
            loads[n][c].wait()

            def some_rows(i, carry):
                row = pl.multiple_of(c * step + i * ROWS, ROWS)
                x = raw_ref[n, pl.ds(row, ROWS)].astype(jnp.float32)
                y = (x * inverse_rms(x) * gain_ref[n]).astype(jnp.bfloat16)
                for group in range(groups):
                    for head in range(heads):
                        at = (group * heads + head) * width
                        first = (n * heads + head) * tokens
                        out_ref[group, pl.ds(first + row, ROWS), :width] = y[:, at : at + width]
                return carry

            lax.fori_loop(0, step // ROWS, some_rows, 0)
    for move in moves:
        move.wait()


def in_hbm(x):
    return pltpu.with_memory_space_constraint(x, pltpu.HBM)


def pack(q, k, v, u, q_gain, k_gain, groups, heads):
    tokens, features = q.shape
    width = features // (groups * heads)
    hbm = pl.BlockSpec(memory_space=pltpu.HBM)
    vmem = pl.BlockSpec(memory_space=pltpu.VMEM)
    return pl.pallas_call(
        pack_kernel,
        in_specs=[hbm] * 6,
        out_specs=vmem,
        out_shape=jax.ShapeDtypeStruct((groups, 2 * heads * tokens, 2 * width), jnp.bfloat16),
        scratch_shapes=[
            pltpu.VMEM((2, tokens, features), jnp.bfloat16),
            pltpu.VMEM((2, 1, features), jnp.float32),
            pltpu.SemaphoreType.DMA((2, CHUNKS)),
            pltpu.SemaphoreType.DMA((2,)),
            pltpu.SemaphoreType.DMA((groups * heads, 2)),
        ],
        compiler_params=pltpu.CompilerParams(vmem_limit_bytes=12 << 20),
        name="pack",
    )(*(in_hbm(x) for x in (q, k, v, u, q_gain[None], k_gain[None])))


def attention_kernel(first_ref, lists_ref, live_ref, in_ref, out_ref, *scratch):
    blocks, span, both = in_ref.shape
    heads = len(scratch) // 2
    width = both // 2
    scale = width ** (-0.5)
    turned, sums, gains_ref = scratch[:heads], scratch[heads:-1], scratch[-1]
    first_head = first_ref[0]
    live = [live_ref[0, first_head + head] for head in range(heads)]

    def place(pair, head):
        return pl.ds((pair * heads + head) * BLK, BLK)

    def parts(row):
        pieces = []
        for _ in range(PARTS):
            pieces.append(row.astype(jnp.bfloat16))
            row = row - pieces[-1].astype(jnp.float32)
        return pieces

    def prepare(j, carry):
        for head in range(heads):
            turned[head][j] = in_ref[j, place(1, head)].T
            sums[head][j] = jnp.zeros((BLK, both), jnp.float32)
        return carry

    lax.fori_loop(0, blocks, prepare, 0)

    def start(b, head, slots):
        q = in_ref[b, place(0, head), :width]
        u = in_ref[b, place(0, head), width:]
        diagonal = (q, u)
        chosen = [lists_ref[b, s, first_head + head] for s in range(slots)]
        rows = jnp.concatenate([in_ref[j, place(1, head)] for j in chosen], axis=0)
        scores = contract(rows[:, :width], q, ((1,), (1,)))
        grads = contract(rows[:, width:], u, ((1,), (1,)))
        products = ([scores[s * BLK : (s + 1) * BLK] for s in range(slots)], [grads[s * BLK : (s + 1) * BLK] for s in range(slots)])
        return q, diagonal, chosen, products

    def softmax(head, products):
        scores, grads = products
        factor = scale * LOG2E
        bias = [jnp.where(s < live[head], 0.0, -jnp.inf) for s in range(len(scores))]
        tops = [jnp.max(s, axis=0, keepdims=True) * factor + x for s, x in zip(scores, bias)]
        top = tops[0]
        for t in tops[1:]:
            top = jnp.maximum(top, t)
        raised = [jnp.exp2(s * factor + (x - top)) for s, x in zip(scores, bias)]
        total = raised[0]
        inner = raised[0] * grads[0]
        for e, g in zip(raised[1:], grads[1:]):
            total = total + e
            inner = inner + e * g
        inverse = 1.0 / jnp.sum(total, axis=0, keepdims=True)
        delta = jnp.sum(inner, axis=0, keepdims=True) * inverse
        probs = [e * inverse for e in raised]
        low = [p.astype(jnp.bfloat16) for p in probs]
        ds = [(p * ((g - delta) * scale)).astype(jnp.bfloat16) for p, g in zip(probs, grads)]
        return low, ds

    def finish_block(b, head, q, diagonal, chosen, low, ds):
        keys = jnp.concatenate([turned[head][j, :width] for j in chosen], axis=1)
        values = jnp.concatenate([turned[head][j, width:] for j in chosen], axis=1)
        out_t = contract(values, jnp.concatenate(low, axis=0), ((1,), (0,)))
        dq_t = contract(keys, jnp.concatenate(ds, axis=0), ((1,), (0,)))
        q, u = diagonal
        more_k = contract(jnp.concatenate(ds, axis=0), q, ((1,), (0,)))
        more_v = contract(jnp.concatenate(low, axis=0), u, ((1,), (0,)))
        old = [sums[head][j] for j in chosen]
        for s, (j, o) in enumerate(zip(chosen, old)):
            sums[head][j, :, :width] = o[:, :width] + more_k[s * BLK : (s + 1) * BLK]
            sums[head][j, :, width:] = o[:, width:] + more_v[s * BLK : (s + 1) * BLK]
        dq = dq_t.T.astype(jnp.bfloat16)
        out_ref[b, place(0, head), :width] = dq
        out_ref[b, place(0, head), width:] = out_t.T.astype(jnp.bfloat16)
        return jnp.sum(dq.astype(jnp.float32) * q.astype(jnp.float32), axis=0, keepdims=True)

    most = live[0]
    for head in range(1, heads):
        most = jnp.maximum(most, live[head])
    for slots in (2, 3, 4):

        @pl.when(most == slots)
        def _():
            def step(b, gain):
                begun = [start(b, h, slots) for h in range(heads)]
                done = []
                for h, (q, diagonal, chosen, products) in enumerate(begun):
                    low, ds = softmax(h, products)
                    done.append(gain[h] + finish_block(b, h, q, diagonal, chosen, low, ds))
                return tuple(done)

            gain = lax.fori_loop(
                0, blocks, step, (jnp.zeros((1, width), jnp.float32),) * heads
            )
            for h in range(heads):
                gains_ref[h : h + 1] = gain[h]

    def finish(j, gain):
        totals = []
        for head in range(heads):
            grads = sums[head][j].astype(jnp.bfloat16)
            out_ref[j, place(1, head)] = grads
            k = in_ref[j, place(1, head), :width].astype(jnp.float32)
            dk = grads[:, :width].astype(jnp.float32)
            totals.append(gain[head] + jnp.sum(dk * k, axis=0, keepdims=True))
        return tuple(totals)

    gain = lax.fori_loop(0, blocks, finish, (jnp.zeros((1, width), jnp.float32),) * heads)
    for h in range(heads):
        gains_ref[heads + h : heads + h + 1] = gain[h]
    extra = []
    for piece in parts(gains_ref[...]):
        for n in range(2):
            rows = [piece[n * heads + h : n * heads + h + 1] for h in range(heads)]
            extra.append(jnp.concatenate(rows, axis=1))
    extra.append(jnp.zeros((SPARE - 2 * PARTS, both), jnp.bfloat16))
    extra = jnp.concatenate(extra, axis=0)

    def spread(j, carry):
        out_ref[j, span:] = extra
        return carry

    lax.fori_loop(0, blocks, spread, 0)


def attention(first, lists, live, arrived, heads):
    blocks, span, both = arrived.shape
    vmem = pl.BlockSpec(memory_space=pltpu.VMEM)
    smem = pl.BlockSpec(memory_space=pltpu.SMEM)
    return pl.pallas_call(
        attention_kernel,
        in_specs=[smem, smem, smem, vmem],
        out_specs=vmem,
        out_shape=jax.ShapeDtypeStruct((blocks, span + SPARE, both), jnp.bfloat16),
        scratch_shapes=[pltpu.VMEM((blocks, both, BLK), jnp.bfloat16)] * heads
        + [pltpu.VMEM((blocks, BLK, both), jnp.float32)] * heads
        + [pltpu.VMEM((2 * heads, both // 2), jnp.float32)],
        compiler_params=pltpu.CompilerParams(vmem_limit_bytes=24 << 20),
        name="attention",
    )(first, lists, live, arrived)


def unpack_kernel(
    back_ref, q_ref, k_ref, qg_ref, kg_ref, out_hbm, dq_hbm, dk_hbm, dv_hbm, done_ref, sems, copy_sems
):
    groups, _, both = back_ref.shape
    width = both // 2
    tokens, features = q_ref.shape
    heads = features // (groups * width)
    step = tokens // CHUNKS
    moves = []
    for group in range(groups):
        for head in range(heads):
            at = (group * heads + head) * width
            for n, hbm in enumerate((out_hbm, dv_hbm)):
                first = (n * heads + head) * tokens
                moves.append(
                    pltpu.make_async_copy(
                        back_ref.at[group, pl.ds(first, tokens), pl.ds(width, width)],
                        hbm.at[:, pl.ds(at, width)],
                        copy_sems.at[group * heads + head, n],
                    )
                )
    for move in moves:
        move.start()
    for c in range(CHUNKS):
        for n, (raw_ref, gain_ref, hbm) in enumerate(
            ((q_ref, qg_ref, dq_hbm), (k_ref, kg_ref, dk_hbm))
        ):

            def some_rows(i, carry):
                row = pl.multiple_of(c * step + i * ROWS, ROWS)
                x = raw_ref[pl.ds(row, ROWS)].astype(jnp.float32)
                inverse = inverse_rms(x)
                unit = x * inverse
                grads = jnp.concatenate(
                    [
                        back_ref[g, pl.ds((n * heads + h) * tokens + row, ROWS), :width]
                        for g in range(groups)
                        for h in range(heads)
                    ],
                    axis=-1,
                )
                g = grads.astype(jnp.float32) * gain_ref[...]
                mean = jnp.mean(g * unit, axis=-1, keepdims=True)
                done_ref[n, pl.ds(row, ROWS)] = (inverse * (g - unit * mean)).astype(jnp.bfloat16)
                return carry

            lax.fori_loop(0, step // ROWS, some_rows, 0)
            move = pltpu.make_async_copy(
                done_ref.at[n, pl.ds(c * step, step)], hbm.at[pl.ds(c * step, step)], sems.at[n, c]
            )
            move.start()
            moves.append(move)
    for move in moves:
        move.wait()


def unpack(back, q, k, q_gain, k_gain):
    groups, _, both = back.shape
    tokens, features = q.shape
    hbm = pl.BlockSpec(memory_space=pltpu.HBM)
    vmem = pl.BlockSpec(memory_space=pltpu.VMEM)
    return pl.pallas_call(
        unpack_kernel,
        in_specs=[vmem] * 5,
        out_specs=[hbm] * 4,
        out_shape=[jax.ShapeDtypeStruct((tokens, features), jnp.bfloat16)] * 4,
        scratch_shapes=[
            pltpu.VMEM((2, tokens, features), jnp.bfloat16),
            pltpu.SemaphoreType.DMA((2, CHUNKS)),
            pltpu.SemaphoreType.DMA((2 * features // both, 2)),
        ],
        compiler_params=pltpu.CompilerParams(vmem_limit_bytes=12 << 20),
        name="unpack",
    )(back, q, k, q_gain[None], k_gain[None])


def gains_kernel(back_ref, out_ref):
    groups, rows, both = back_ref.shape
    span = rows - SPARE
    for group in range(groups):
        extra = back_ref[group, span:].astype(jnp.float32)
        total = extra[0:2]
        for n in range(1, PARTS):
            total = total + extra[2 * n : 2 * n + 2]
        out_ref[:, group * both : (group + 1) * both] = total


def add_kernel(a_ref, b_ref, out_ref):
    out_ref[...] = a_ref[...] + b_ref[...]


def last_kernel(a_ref, b_ref, qg_ref, kg_ref, q_ref, k_ref):
    total = a_ref[...] + b_ref[...]
    q_ref[...] = total[0:1] / qg_ref[...]
    k_ref[...] = total[1:2] / kg_ref[...]


def small_call(kernel, shapes, name, *args):
    return pl.pallas_call(
        kernel,
        in_specs=[pl.BlockSpec(memory_space=pltpu.VMEM)] * len(args),
        out_specs=[pl.BlockSpec(memory_space=pltpu.VMEM)] * len(shapes),
        out_shape=[jax.ShapeDtypeStruct(shape, jnp.float32) for shape in shapes],
        compiler_params=pltpu.CompilerParams(vmem_limit_bytes=2 << 20),
        name=name,
    )(*args)


def clip_gains(back, q_gain, k_gain):
    features = q_gain.shape[0]
    (total,) = small_call(gains_kernel, [(2, features)], "gains", back)
    size = lax.axis_size("clip")
    flips = [1, 2, 6]
    for n, flip in enumerate(flips):
        other = lax.ppermute(total, "clip", [(i, i ^ flip) for i in range(size)])
        if n < len(flips) - 1:
            (total,) = small_call(add_kernel, [(2, features)], "add", total, other)
    q, k = small_call(
        last_kernel, [(1, features)] * 2, "last", total, other, q_gain[None], k_gain[None]
    )
    return q[0], k[0]


def shards(query_raw, key_raw, value, upstream, query_gain, key_gain, key_blocks, live):
    groups = lax.axis_size("seq")
    heads = key_blocks.shape[1] // groups
    first = (lax.axis_index("seq") * heads).reshape(1)
    lists = jnp.transpose(key_blocks[0], (1, 2, 0))
    packed = pack(
        query_raw[0], key_raw[0], value[0], upstream[0], query_gain, key_gain, groups, heads
    )
    packed, first = lax.optimization_barrier((packed, first))
    arrived = lax.all_to_all(packed, "seq", split_axis=0, concat_axis=0, tiled=True)
    results = attention(first, lists, live, arrived, heads)
    back = lax.all_to_all(results, "seq", split_axis=0, concat_axis=0, tiled=True)
    attended, grad_query, grad_key, grad_value = unpack(
        back, query_raw[0], key_raw[0], query_gain, key_gain
    )
    q_total, k_total = clip_gains(back, query_gain, key_gain)
    return (
        attended[None],
        grad_query[None],
        grad_key[None],
        grad_value[None],
        q_total,
        k_total,
    )


def solution(mesh):
    tokens = P("clip", "seq", None)
    return jax.shard_map(
        shards,
        mesh=mesh,
        in_specs=(tokens,) * 4 + (P(), P(), P("clip", None, None, None), P("clip", None)),
        out_specs=(tokens,) * 4 + (P(), P()),
        check_vma=False,
    )
```

```python
import jax
import jax.numpy as jnp
from jax import lax
from jax.experimental import pallas as pl
from jax.experimental.pallas import tpu as pltpu
from jax.sharding import PartitionSpec as P

BLK = 128
EPSILON = 1e-06
ROWS = 16
CHUNKS = 4
PARTS = 3
SPARE = 8
QUERY, COTANGENT, KEY, VALUE = range(4)
GRAD_Q, OUT, GRAD_K, GRAD_V = range(4)
LOG2E = 1.4426950408889634


def contract(a, b, dims):
    return lax.dot_general(a, b, (dims, ((), ())), preferred_element_type=jnp.float32)


def inverse_rms(x):
    return lax.rsqrt(jnp.mean(x * x, axis=-1, keepdims=True) + EPSILON)


def pack_kernel(
    q_hbm, k_hbm, v_hbm, u_hbm, qg_hbm, kg_hbm, out_ref, raw_ref, gain_ref, raw_sems, gain_sems, copy_sems
):
    groups, span, both = out_ref.shape
    width = both // 2
    tokens = raw_ref.shape[1]
    heads = span // (2 * tokens)
    step = tokens // CHUNKS

    loads = [
        [
            pltpu.make_async_copy(
                hbm.at[pl.ds(c * step, step)],
                raw_ref.at[n, pl.ds(c * step, step)],
                raw_sems.at[n, c],
            )
            for c in range(CHUNKS)
        ]
        for n, hbm in enumerate((q_hbm, k_hbm))
    ]
    gain_loads = [
        pltpu.make_async_copy(hbm, gain_ref.at[n], gain_sems.at[n])
        for n, hbm in enumerate((qg_hbm, kg_hbm))
    ]
    for n in range(2):
        gain_loads[n].start()
        loads[n][0].start()
    for c in range(1, CHUNKS):
        for n in range(2):
            loads[n][c].start()
    moves = []
    for group in range(groups):
        for head in range(heads):
            at = (group * heads + head) * width
            for n, (hbm, pair) in enumerate(((u_hbm, 0), (v_hbm, 1))):
                first = (pair * heads + head) * tokens
                moves.append(
                    pltpu.make_async_copy(
                        hbm.at[:, pl.ds(at, width)],
                        out_ref.at[group, pl.ds(first, tokens), pl.ds(width, width)],
                        copy_sems.at[group * heads + head, n],
                    )
                )
    for move in moves:
        move.start()
    for c in range(CHUNKS):
        for n in range(2):
            if c == 0:
                gain_loads[n].wait()
            loads[n][c].wait()

            def some_rows(i, carry):
                row = pl.multiple_of(c * step + i * ROWS, ROWS)
                x = raw_ref[n, pl.ds(row, ROWS)].astype(jnp.float32)
                y = (x * inverse_rms(x) * gain_ref[n]).astype(jnp.bfloat16)
                for group in range(groups):
                    for head in range(heads):
                        at = (group * heads + head) * width
                        first = (n * heads + head) * tokens
                        out_ref[group, pl.ds(first + row, ROWS), :width] = y[:, at : at + width]
                return carry

            lax.fori_loop(0, step // ROWS, some_rows, 0)
    for move in moves:
        move.wait()


def in_hbm(x):
    return pltpu.with_memory_space_constraint(x, pltpu.HBM)


def pack(q, k, v, u, q_gain, k_gain, groups, heads):
    tokens, features = q.shape
    width = features // (groups * heads)
    hbm = pl.BlockSpec(memory_space=pltpu.HBM)
    vmem = pl.BlockSpec(memory_space=pltpu.VMEM)
    return pl.pallas_call(
        pack_kernel,
        in_specs=[hbm] * 6,
        out_specs=vmem,
        out_shape=jax.ShapeDtypeStruct((groups, 2 * heads * tokens, 2 * width), jnp.bfloat16),
        scratch_shapes=[
            pltpu.VMEM((2, tokens, features), jnp.bfloat16),
            pltpu.VMEM((2, 1, features), jnp.float32),
            pltpu.SemaphoreType.DMA((2, CHUNKS)),
            pltpu.SemaphoreType.DMA((2,)),
            pltpu.SemaphoreType.DMA((groups * heads, 2)),
        ],
        compiler_params=pltpu.CompilerParams(vmem_limit_bytes=12 << 20),
        name="pack",
    )(*(in_hbm(x) for x in (q, k, v, u, q_gain[None], k_gain[None])))


def attention_kernel(first_ref, lists_ref, live_ref, in_ref, out_ref, *scratch):
    blocks, span, both = in_ref.shape
    heads = len(scratch) // 3
    width = both // 2
    scale = width ** (-0.5)
    turned, sums, ahead, gains_ref = scratch[:heads], scratch[heads : 2 * heads], scratch[2 * heads : -1], scratch[-1]
    first_head = first_ref[0]
    live = [live_ref[0, first_head + head] for head in range(heads)]

    def place(pair, head):
        return pl.ds((pair * heads + head) * BLK, BLK)

    def parts(row):
        pieces = []
        for _ in range(PARTS):
            pieces.append(row.astype(jnp.bfloat16))
            row = row - pieces[-1].astype(jnp.float32)
        return pieces

    def prepare(j, carry):
        for head in range(heads):
            turned[head][j] = in_ref[j, place(1, head)].T
            sums[head][j] = jnp.zeros((BLK, both), jnp.float32)
        return carry

    lax.fori_loop(0, blocks, prepare, 0)

    def start(b, head, slots):
        q = in_ref[b, place(0, head), :width]
        u = in_ref[b, place(0, head), width:]
        diagonal = (q, u)
        chosen = [lists_ref[b, s, first_head + head] for s in range(slots)]
        rows = jnp.concatenate([in_ref[j, place(1, head)] for j in chosen], axis=0)
        scores = contract(rows[:, :width], q, ((1,), (1,)))
        grads = contract(rows[:, width:], u, ((1,), (1,)))
        products = ([scores[s * BLK : (s + 1) * BLK] for s in range(slots)], [grads[s * BLK : (s + 1) * BLK] for s in range(slots)])
        return q, diagonal, chosen, products

    def softmax(head, products):
        scores, grads = products
        factor = scale * LOG2E
        bias = [jnp.where(s < live[head], 0.0, -jnp.inf) for s in range(len(scores))]
        tops = [jnp.max(s, axis=0, keepdims=True) * factor + x for s, x in zip(scores, bias)]
        top = tops[0]
        for t in tops[1:]:
            top = jnp.maximum(top, t)
        raised = [jnp.exp2(s * factor + (x - top)) for s, x in zip(scores, bias)]
        total = raised[0]
        inner = raised[0] * grads[0]
        for e, g in zip(raised[1:], grads[1:]):
            total = total + e
            inner = inner + e * g
        inverse = 1.0 / jnp.sum(total, axis=0, keepdims=True)
        delta = jnp.sum(inner, axis=0, keepdims=True) * inverse
        probs = [e * inverse for e in raised]
        low = [p.astype(jnp.bfloat16) for p in probs]
        ds = [(p * ((g - delta) * scale)).astype(jnp.bfloat16) for p, g in zip(probs, grads)]
        return low, ds

    def finish_block(b, head, q, diagonal, chosen, low, ds):
        keys = jnp.concatenate([turned[head][j, :width] for j in chosen], axis=1)
        values = jnp.concatenate([turned[head][j, width:] for j in chosen], axis=1)
        out_t = contract(values, jnp.concatenate(low, axis=0), ((1,), (0,)))
        dq_t = contract(keys, jnp.concatenate(ds, axis=0), ((1,), (0,)))
        q, u = diagonal
        more_k = contract(jnp.concatenate(ds, axis=0), q, ((1,), (0,)))
        more_v = contract(jnp.concatenate(low, axis=0), u, ((1,), (0,)))
        old = [sums[head][j] for j in chosen]
        for s, (j, o) in enumerate(zip(chosen, old)):
            sums[head][j, :, :width] = o[:, :width] + more_k[s * BLK : (s + 1) * BLK]
            sums[head][j, :, width:] = o[:, width:] + more_v[s * BLK : (s + 1) * BLK]
        dq = dq_t.T.astype(jnp.bfloat16)
        out_ref[b, place(0, head), :width] = dq
        out_ref[b, place(0, head), width:] = out_t.T.astype(jnp.bfloat16)
        return jnp.sum(dq.astype(jnp.float32) * q.astype(jnp.float32), axis=0, keepdims=True)

    most = live[0]
    for head in range(1, heads):
        most = jnp.maximum(most, live[head])
    for slots in (2, 3, 4):

        @pl.when(most == slots)
        def _():
            def keep(h, products):
                for s in range(slots):
                    for n in range(2):
                        ahead[h][n, s] = products[n][s]

            def step(b, gain):
                done = []
                for h in range(heads):
                    products = [[ahead[h][n, s] for s in range(slots)] for n in range(2)]
                    after = h + 1 if h + 1 < heads else 0
                    at = b if h + 1 < heads else jnp.minimum(b + 1, blocks - 1)
                    keep(after, start(at, after, slots)[3])
                    low, ds = softmax(h, products)
                    q = in_ref[b, place(0, h), :width]
                    u = in_ref[b, place(0, h), width:]
                    chosen = [lists_ref[b, s, first_head + h] for s in range(slots)]
                    done.append(gain[h] + finish_block(b, h, q, (q, u), chosen, low, ds))
                return tuple(done)

            keep(0, start(0, 0, slots)[3])

            gain = lax.fori_loop(
                0, blocks, step, (jnp.zeros((1, width), jnp.float32),) * heads
            )
            for h in range(heads):
                gains_ref[h : h + 1] = gain[h]

    extra = parts(jnp.concatenate([gains_ref[h : h + 1] for h in range(heads)], axis=1))
    extra.append(jnp.zeros((SPARE - PARTS, both), jnp.bfloat16))
    extra = jnp.concatenate(extra, axis=0)

    def finish(j, carry):
        for head in range(heads):
            out_ref[j, place(1, head)] = sums[head][j].astype(jnp.bfloat16)
        out_ref[j, span:] = extra
        return carry

    lax.fori_loop(0, blocks, finish, 0)


def attention(first, lists, live, arrived, heads):
    blocks, span, both = arrived.shape
    vmem = pl.BlockSpec(memory_space=pltpu.VMEM)
    smem = pl.BlockSpec(memory_space=pltpu.SMEM)
    return pl.pallas_call(
        attention_kernel,
        in_specs=[smem, smem, smem, vmem],
        out_specs=vmem,
        out_shape=jax.ShapeDtypeStruct((blocks, span + SPARE, both), jnp.bfloat16),
        scratch_shapes=[pltpu.VMEM((blocks, both, BLK), jnp.bfloat16)] * heads
        + [pltpu.VMEM((blocks, BLK, both), jnp.float32)] * heads
        + [pltpu.VMEM((2, lists.shape[1], BLK, BLK), jnp.float32)] * heads
        + [pltpu.VMEM((heads, both // 2), jnp.float32)],
        compiler_params=pltpu.CompilerParams(vmem_limit_bytes=24 << 20),
        name="attention",
    )(first, lists, live, arrived)


def unpack_kernel(
    back_ref, q_ref, k_ref, qg_ref, kg_ref, out_hbm, dq_hbm, dk_hbm, dv_hbm, done_ref, sems, copy_sems
):
    groups, _, both = back_ref.shape
    width = both // 2
    tokens, features = q_ref.shape
    heads = features // (groups * width)
    step = tokens // CHUNKS
    moves = []
    for group in range(groups):
        for head in range(heads):
            at = (group * heads + head) * width
            for n, hbm in enumerate((out_hbm, dv_hbm)):
                first = (n * heads + head) * tokens
                moves.append(
                    pltpu.make_async_copy(
                        back_ref.at[group, pl.ds(first, tokens), pl.ds(width, width)],
                        hbm.at[:, pl.ds(at, width)],
                        copy_sems.at[group * heads + head, n],
                    )
                )
    for move in moves:
        move.start()
    for c in range(CHUNKS):
        for n, (raw_ref, gain_ref, hbm) in enumerate(
            ((q_ref, qg_ref, dq_hbm), (k_ref, kg_ref, dk_hbm))
        ):

            def some_rows(i, carry):
                row = pl.multiple_of(c * step + i * ROWS, ROWS)
                x = raw_ref[pl.ds(row, ROWS)].astype(jnp.float32)
                inverse = inverse_rms(x)
                unit = x * inverse
                grads = jnp.concatenate(
                    [
                        back_ref[g, pl.ds((n * heads + h) * tokens + row, ROWS), :width]
                        for g in range(groups)
                        for h in range(heads)
                    ],
                    axis=-1,
                )
                g = grads.astype(jnp.float32) * gain_ref[...]
                mean = jnp.mean(g * unit, axis=-1, keepdims=True)
                done_ref[n, pl.ds(row, ROWS)] = (inverse * (g - unit * mean)).astype(jnp.bfloat16)
                return carry

            lax.fori_loop(0, step // ROWS, some_rows, 0)
            move = pltpu.make_async_copy(
                done_ref.at[n, pl.ds(c * step, step)], hbm.at[pl.ds(c * step, step)], sems.at[n, c]
            )
            move.start()
            moves.append(move)
    for move in moves:
        move.wait()


def unpack(back, q, k, q_gain, k_gain):
    groups, _, both = back.shape
    tokens, features = q.shape
    hbm = pl.BlockSpec(memory_space=pltpu.HBM)
    vmem = pl.BlockSpec(memory_space=pltpu.VMEM)
    return pl.pallas_call(
        unpack_kernel,
        in_specs=[vmem] * 5,
        out_specs=[hbm] * 4,
        out_shape=[jax.ShapeDtypeStruct((tokens, features), jnp.bfloat16)] * 4,
        scratch_shapes=[
            pltpu.VMEM((2, tokens, features), jnp.bfloat16),
            pltpu.SemaphoreType.DMA((2, CHUNKS)),
            pltpu.SemaphoreType.DMA((2 * features // both, 2)),
        ],
        compiler_params=pltpu.CompilerParams(vmem_limit_bytes=12 << 20),
        name="unpack",
    )(back, q, k, q_gain[None], k_gain[None])


def gains_kernel(back_ref, out_ref):
    groups, rows, both = back_ref.shape
    lanes = out_ref.shape[1]
    for group in range(groups):
        extra = back_ref[group, rows - SPARE :].astype(jnp.float32)
        total = extra[0:1]
        for n in range(1, PARTS):
            total = total + extra[n : n + 1]
        for n in range(both // lanes):
            row = total[:, n * lanes : (n + 1) * lanes]
            at = group * (both // lanes) + n
            out_ref[at : at + 1] = row


def add_kernel(a_ref, b_ref, out_ref):
    out_ref[...] = a_ref[...] + b_ref[...]


def last_kernel(a_ref, b_ref, qg_ref, kg_ref, q_ref, k_ref):
    total = a_ref[...] + b_ref[...]
    q_ref[...] = total / qg_ref[...]
    k_ref[...] = total / kg_ref[...]


def small_call(kernel, shapes, name, *args):
    return pl.pallas_call(
        kernel,
        in_specs=[pl.BlockSpec(memory_space=pltpu.VMEM)] * len(args),
        out_specs=[pl.BlockSpec(memory_space=pltpu.VMEM)] * len(shapes),
        out_shape=[jax.ShapeDtypeStruct(shape, jnp.float32) for shape in shapes],
        compiler_params=pltpu.CompilerParams(vmem_limit_bytes=2 << 20),
        name=name,
    )(*args)


def clip_gains(back, q_gain, k_gain):
    size = lax.axis_size("clip")
    rows = q_gain.shape[0] // BLK
    (total,) = small_call(gains_kernel, [(rows, BLK)], "gains", back)
    flips = [1, 2, 6]
    for n, flip in enumerate(flips):
        other = lax.ppermute(total, "clip", [(i, i ^ flip) for i in range(size)])
        if n < len(flips) - 1:
            (total,) = small_call(add_kernel, [(rows, BLK)], "add", total, other)
    q, k = small_call(
        last_kernel,
        [(rows, BLK)] * 2,
        "last",
        total,
        other,
        q_gain.reshape(rows, BLK),
        k_gain.reshape(rows, BLK),
    )
    return q.reshape(-1), k.reshape(-1)


def shards(query_raw, key_raw, value, upstream, query_gain, key_gain, key_blocks, live):
    groups = lax.axis_size("seq")
    heads = key_blocks.shape[1] // groups
    first = (lax.axis_index("seq") * heads).reshape(1)
    lists = jnp.transpose(key_blocks[0], (1, 2, 0))
    packed = pack(
        query_raw[0], key_raw[0], value[0], upstream[0], query_gain, key_gain, groups, heads
    )
    packed, first = lax.optimization_barrier((packed, first))
    arrived = lax.all_to_all(packed, "seq", split_axis=0, concat_axis=0, tiled=True)
    results = attention(first, lists, live, arrived, heads)
    back = lax.all_to_all(results, "seq", split_axis=0, concat_axis=0, tiled=True)
    attended, grad_query, grad_key, grad_value = unpack(
        back, query_raw[0], key_raw[0], query_gain, key_gain
    )
    q_total, k_total = clip_gains(back, query_gain, key_gain)
    return (
        attended[None],
        grad_query[None],
        grad_key[None],
        grad_value[None],
        q_total,
        k_total,
    )


def solution(mesh):
    tokens = P("clip", "seq", None)
    return jax.shard_map(
        shards,
        mesh=mesh,
        in_specs=(tokens,) * 4 + (P(), P(), P("clip", None, None, None), P("clip", None)),
        out_specs=(tokens,) * 4 + (P(), P()),
        check_vma=False,
    )
```

```python
import jax
import jax.numpy as jnp
from jax import lax
from jax.experimental import pallas as pl
from jax.experimental.pallas import tpu as pltpu
from jax.sharding import PartitionSpec as P

BLK = 128
EPSILON = 1e-06
ROWS = 16
CHUNKS = 4
PARTS = 3
SPARE = 8
QUERY, COTANGENT, KEY, VALUE = range(4)
GRAD_Q, OUT, GRAD_K, GRAD_V = range(4)
LOG2E = 1.4426950408889634


def contract(a, b, dims):
    return lax.dot_general(a, b, (dims, ((), ())), preferred_element_type=jnp.float32)


def inverse_rms(x):
    return lax.rsqrt(jnp.mean(x * x, axis=-1, keepdims=True) + EPSILON)


def rank_heads(live_ref, place_ref, order_ref):
    count = place_ref.shape[0]
    most = lax.fori_loop(0, count, lambda h, n: n + (live_ref[0, h] >= 4).astype(jnp.int32), 0)
    some = lax.fori_loop(0, count, lambda h, n: n + (live_ref[0, h] >= 3).astype(jnp.int32), 0)

    def put(h, counts):
        four, three, two = counts
        is_four = live_ref[0, h] >= 4
        is_three = jnp.logical_and(live_ref[0, h] >= 3, jnp.logical_not(is_four))
        rank = jnp.where(is_four, four, jnp.where(is_three, three, two))
        place_ref[h] = rank
        order_ref[rank] = h
        step = jnp.logical_not(jnp.logical_or(is_four, is_three))
        return (
            four + is_four.astype(jnp.int32),
            three + is_three.astype(jnp.int32),
            two + step.astype(jnp.int32),
        )

    lax.fori_loop(0, count, put, (jnp.int32(0), most, some))


def group_and_slot(rank, groups):
    second = rank >= groups
    return jnp.where(second, 2 * groups - 1 - rank, rank), second.astype(jnp.int32)


def rank_scratch(heads):
    return [pltpu.SMEM((heads,), jnp.int32)] * 2


def pack_kernel(
    live_hbm,
    q_hbm,
    k_hbm,
    v_hbm,
    u_hbm,
    qg_hbm,
    kg_hbm,
    out_ref,
    raw_ref,
    gain_ref,
    live_ref,
    place_ref,
    order_ref,
    raw_sems,
    gain_sems,
    copy_sems,
    live_sem,
):
    groups, span, both = out_ref.shape
    width = both // 2
    tokens = raw_ref.shape[1]
    heads = span // (2 * tokens)
    step = tokens // CHUNKS

    loads = [
        [
            pltpu.make_async_copy(
                hbm.at[pl.ds(c * step, step)],
                raw_ref.at[n, pl.ds(c * step, step)],
                raw_sems.at[n, c],
            )
            for c in range(CHUNKS)
        ]
        for n, hbm in enumerate((q_hbm, k_hbm))
    ]
    gain_loads = [
        pltpu.make_async_copy(hbm, gain_ref.at[n], gain_sems.at[n])
        for n, hbm in enumerate((qg_hbm, kg_hbm))
    ]
    live_load = pltpu.make_async_copy(live_hbm, live_ref, live_sem)
    live_load.start()
    for n in range(2):
        gain_loads[n].start()
        loads[n][0].start()
    for c in range(1, CHUNKS):
        for n in range(2):
            loads[n][c].start()
    live_load.wait()
    rank_heads(live_ref, place_ref, order_ref)
    moves, spots = [], []
    for head in range(groups * heads):
        group, slot = group_and_slot(place_ref[head], groups)
        spots.append((group, slot))
        for n, (hbm, pair) in enumerate(((u_hbm, 0), (v_hbm, 1))):
            first = pl.multiple_of((pair * heads + slot) * tokens, tokens)
            moves.append(
                pltpu.make_async_copy(
                    hbm.at[:, pl.ds(head * width, width)],
                    out_ref.at[group, pl.ds(first, tokens), pl.ds(width, width)],
                    copy_sems.at[head, n],
                )
            )
    for move in moves:
        move.start()
    for c in range(CHUNKS):
        for n in range(2):
            if c == 0:
                gain_loads[n].wait()
            loads[n][c].wait()

            def some_rows(i, carry):
                row = pl.multiple_of(c * step + i * ROWS, ROWS)
                x = raw_ref[n, pl.ds(row, ROWS)].astype(jnp.float32)
                y = (x * inverse_rms(x) * gain_ref[n]).astype(jnp.bfloat16)
                for head, (group, slot) in enumerate(spots):
                    first = pl.multiple_of((n * heads + slot) * tokens + row, ROWS)
                    at = head * width
                    out_ref[group, pl.ds(first, ROWS), :width] = y[:, at : at + width]
                return carry

            lax.fori_loop(0, step // ROWS, some_rows, 0)
    for move in moves:
        move.wait()


def in_hbm(x):
    return pltpu.with_memory_space_constraint(x, pltpu.HBM)


def pack(live, q, k, v, u, q_gain, k_gain, groups, heads):
    tokens, features = q.shape
    width = features // (groups * heads)
    hbm = pl.BlockSpec(memory_space=pltpu.HBM)
    vmem = pl.BlockSpec(memory_space=pltpu.VMEM)
    return pl.pallas_call(
        pack_kernel,
        in_specs=[hbm] * 7,
        out_specs=vmem,
        out_shape=jax.ShapeDtypeStruct((groups, 2 * heads * tokens, 2 * width), jnp.bfloat16),
        scratch_shapes=[
            pltpu.VMEM((2, tokens, features), jnp.bfloat16),
            pltpu.VMEM((2, 1, features), jnp.float32),
            pltpu.SMEM(live.shape, jnp.int32),
            *rank_scratch(groups * heads),
            pltpu.SemaphoreType.DMA((2, CHUNKS)),
            pltpu.SemaphoreType.DMA((2,)),
            pltpu.SemaphoreType.DMA((groups * heads, 2)),
            pltpu.SemaphoreType.DMA(()),
        ],
        compiler_params=pltpu.CompilerParams(vmem_limit_bytes=12 << 20),
        name="pack",
    )(*(in_hbm(x) for x in (live, q, k, v, u, q_gain[None], k_gain[None])))


def attention_kernel(mine_ref, lists_ref, live_ref, in_ref, out_ref, *scratch):
    place_ref, order_ref, *scratch = scratch
    blocks, span, both = in_ref.shape
    heads = len(scratch) // 3
    width = both // 2
    scale = width ** (-0.5)
    turned, sums, ahead, gains_ref = scratch[:heads], scratch[heads : 2 * heads], scratch[2 * heads : -1], scratch[-1]
    rank_heads(live_ref, place_ref, order_ref)
    mine = mine_ref[0]
    owned = [order_ref[mine], order_ref[2 * blocks - 1 - mine]]
    live = [live_ref[0, h] for h in owned]

    def place(pair, head):
        return pl.ds((pair * heads + head) * BLK, BLK)

    def parts(row):
        pieces = []
        for _ in range(PARTS):
            pieces.append(row.astype(jnp.bfloat16))
            row = row - pieces[-1].astype(jnp.float32)
        return pieces

    def prepare(j, carry):
        for head in range(heads):
            turned[head][j] = in_ref[j, place(1, head)].T
            sums[head][j] = jnp.zeros((BLK, both), jnp.float32)
        return carry

    lax.fori_loop(0, blocks, prepare, 0, unroll=4)

    def start(b, head, slots):
        q = in_ref[b, place(0, head), :width]
        u = in_ref[b, place(0, head), width:]
        diagonal = (q, u)
        chosen = [lists_ref[b, s, owned[head]] for s in range(slots)]
        rows = jnp.concatenate([in_ref[j, place(1, head)] for j in chosen], axis=0)
        scores = contract(rows[:, :width], q, ((1,), (1,)))
        grads = contract(rows[:, width:], u, ((1,), (1,)))
        products = ([scores[s * BLK : (s + 1) * BLK] for s in range(slots)], [grads[s * BLK : (s + 1) * BLK] for s in range(slots)])
        return q, diagonal, chosen, products

    def softmax(products):
        scores, grads = products
        factor = scale * LOG2E
        tops = [jnp.max(s, axis=0, keepdims=True) * factor for s in scores]
        top = tops[0]
        for t in tops[1:]:
            top = jnp.maximum(top, t)
        raised = [jnp.exp2(s * factor - top) for s in scores]
        total = raised[0]
        inner = raised[0] * grads[0]
        for e, g in zip(raised[1:], grads[1:]):
            total = total + e
            inner = inner + e * g
        inverse = 1.0 / jnp.sum(total, axis=0, keepdims=True)
        delta = jnp.sum(inner, axis=0, keepdims=True) * inverse
        probs = [e * inverse for e in raised]
        low = [p.astype(jnp.bfloat16) for p in probs]
        ds = [(p * ((g - delta) * scale)).astype(jnp.bfloat16) for p, g in zip(probs, grads)]
        return low, ds

    def finish_block(b, head, q, diagonal, chosen, low, ds):
        keys = jnp.concatenate([turned[head][j, :width] for j in chosen], axis=1)
        values = jnp.concatenate([turned[head][j, width:] for j in chosen], axis=1)
        out_t = contract(values, jnp.concatenate(low, axis=0), ((1,), (0,)))
        dq_t = contract(keys, jnp.concatenate(ds, axis=0), ((1,), (0,)))
        q, u = diagonal
        more_k = contract(jnp.concatenate(ds, axis=0), q, ((1,), (0,)))
        more_v = contract(jnp.concatenate(low, axis=0), u, ((1,), (0,)))
        old = [sums[head][j] for j in chosen]
        for s, (j, o) in enumerate(zip(chosen, old)):
            sums[head][j, :, :width] = o[:, :width] + more_k[s * BLK : (s + 1) * BLK]
            sums[head][j, :, width:] = o[:, width:] + more_v[s * BLK : (s + 1) * BLK]
        dq = dq_t.astype(jnp.bfloat16).T
        out_ref[b, place(0, head), :width] = dq
        out_ref[b, place(0, head), width:] = out_t.astype(jnp.bfloat16).T
        return jnp.sum(dq.astype(jnp.float32) * q.astype(jnp.float32), axis=0, keepdims=True)

    for slots in ((2, 2), (3, 2), (3, 3), (4, 2), (4, 3), (4, 4)):

        @pl.when(jnp.logical_and(live[0] == slots[0], live[1] == slots[1]))
        def _():
            def keep(h, products):
                for s in range(slots[h]):
                    for n in range(2):
                        ahead[h][n, s] = products[n][s]

            def step(b, gain):
                done = []
                for h in range(heads):
                    products = [[ahead[h][n, s] for s in range(slots[h])] for n in range(2)]
                    after = h + 1 if h + 1 < heads else 0
                    at = b if h + 1 < heads else jnp.minimum(b + 1, blocks - 1)
                    keep(after, start(at, after, slots[after])[3])
                    low, ds = softmax(products)
                    q = in_ref[b, place(0, h), :width]
                    u = in_ref[b, place(0, h), width:]
                    chosen = [lists_ref[b, s, owned[h]] for s in range(slots[h])]
                    done.append(gain[h] + finish_block(b, h, q, (q, u), chosen, low, ds))
                return tuple(done)

            keep(0, start(0, 0, slots[0])[3])

            gain = lax.fori_loop(
                0, blocks, step, (jnp.zeros((1, width), jnp.float32),) * heads, unroll=4
            )
            for h in range(heads):
                gains_ref[h : h + 1] = gain[h]

    extra = parts(jnp.concatenate([gains_ref[h : h + 1] for h in range(heads)], axis=1))
    extra.append(jnp.zeros((SPARE - PARTS, both), jnp.bfloat16))
    extra = jnp.concatenate(extra, axis=0)

    def finish(j, carry):
        for head in range(heads):
            out_ref[j, place(1, head)] = sums[head][j].astype(jnp.bfloat16)
        out_ref[j, span:] = extra
        return carry

    lax.fori_loop(0, blocks, finish, 0, unroll=4)


def attention(mine, lists, live, arrived, heads):
    blocks, span, both = arrived.shape
    vmem = pl.BlockSpec(memory_space=pltpu.VMEM)
    smem = pl.BlockSpec(memory_space=pltpu.SMEM)
    return pl.pallas_call(
        attention_kernel,
        in_specs=[smem, smem, smem, vmem],
        out_specs=vmem,
        out_shape=jax.ShapeDtypeStruct((blocks, span + SPARE, both), jnp.bfloat16),
        scratch_shapes=rank_scratch(live.shape[1])
        + [pltpu.VMEM((blocks, both, BLK), jnp.bfloat16)] * heads
        + [pltpu.VMEM((blocks, BLK, both), jnp.float32)] * heads
        + [pltpu.VMEM((2, lists.shape[1], BLK, BLK), jnp.float32)] * heads
        + [pltpu.VMEM((heads, both // 2), jnp.float32)],
        compiler_params=pltpu.CompilerParams(vmem_limit_bytes=24 << 20),
        name="attention",
    )(mine, lists, live, arrived)


def unpack_kernel(
    live_ref,
    back_ref,
    q_ref,
    k_ref,
    qg_ref,
    kg_ref,
    out_hbm,
    dq_hbm,
    dk_hbm,
    dv_hbm,
    place_ref,
    order_ref,
    done_ref,
    sems,
    copy_sems,
):
    groups, _, both = back_ref.shape
    width = both // 2
    tokens, features = q_ref.shape
    heads = features // (groups * width)
    step = tokens // CHUNKS
    rank_heads(live_ref, place_ref, order_ref)
    moves, spots = [], []
    for head in range(groups * heads):
        group, slot = group_and_slot(place_ref[head], groups)
        spots.append((group, slot))
        for n, hbm in enumerate((out_hbm, dv_hbm)):
            first = pl.multiple_of((n * heads + slot) * tokens, tokens)
            moves.append(
                pltpu.make_async_copy(
                    back_ref.at[group, pl.ds(first, tokens), pl.ds(width, width)],
                    hbm.at[:, pl.ds(head * width, width)],
                    copy_sems.at[head, n],
                )
            )
    for move in moves:
        move.start()
    for c in range(CHUNKS):
        for n, (raw_ref, gain_ref, hbm) in enumerate(
            ((q_ref, qg_ref, dq_hbm), (k_ref, kg_ref, dk_hbm))
        ):

            def some_rows(i, carry):
                row = pl.multiple_of(c * step + i * ROWS, ROWS)
                x = raw_ref[pl.ds(row, ROWS)].astype(jnp.float32)
                inverse = inverse_rms(x)
                unit = x * inverse
                pieces = []
                for group, slot in spots:
                    first = pl.multiple_of((n * heads + slot) * tokens + row, ROWS)
                    pieces.append(back_ref[group, pl.ds(first, ROWS), :width])
                grads = jnp.concatenate(pieces, axis=-1)
                g = grads.astype(jnp.float32) * gain_ref[...]
                mean = jnp.mean(g * unit, axis=-1, keepdims=True)
                done_ref[n, pl.ds(row, ROWS)] = (inverse * (g - unit * mean)).astype(jnp.bfloat16)
                return carry

            lax.fori_loop(0, step // ROWS, some_rows, 0)
            move = pltpu.make_async_copy(
                done_ref.at[n, pl.ds(c * step, step)], hbm.at[pl.ds(c * step, step)], sems.at[n, c]
            )
            move.start()
            moves.append(move)
    for move in moves:
        move.wait()


def unpack(live, back, q, k, q_gain, k_gain):
    groups, _, both = back.shape
    tokens, features = q.shape
    hbm = pl.BlockSpec(memory_space=pltpu.HBM)
    vmem = pl.BlockSpec(memory_space=pltpu.VMEM)
    return pl.pallas_call(
        unpack_kernel,
        in_specs=[pl.BlockSpec(memory_space=pltpu.SMEM)] + [vmem] * 5,
        out_specs=[hbm] * 4,
        out_shape=[jax.ShapeDtypeStruct((tokens, features), jnp.bfloat16)] * 4,
        scratch_shapes=[
            *rank_scratch(live.shape[1]),
            pltpu.VMEM((2, tokens, features), jnp.bfloat16),
            pltpu.SemaphoreType.DMA((2, CHUNKS)),
            pltpu.SemaphoreType.DMA((2 * features // both, 2)),
        ],
        compiler_params=pltpu.CompilerParams(vmem_limit_bytes=12 << 20),
        name="unpack",
    )(live, back, q, k, q_gain[None], k_gain[None])


def gains_kernel(live_ref, back_ref, out_ref, place_ref, order_ref):
    groups, rows, _ = back_ref.shape
    heads, width = out_ref.shape
    rank_heads(live_ref, place_ref, order_ref)
    for head in range(heads):
        group, slot = group_and_slot(place_ref[head], groups)
        extra = back_ref[group, rows - SPARE :].astype(jnp.float32)
        total = extra[0:1]
        for n in range(1, PARTS):
            total = total + extra[n : n + 1]
        out_ref[head : head + 1] = jnp.where(slot == 0, total[:, :width], total[:, width:])


def add_kernel(a_ref, b_ref, out_ref):
    out_ref[...] = a_ref[...] + b_ref[...]


def last_kernel(a_ref, b_ref, qg_ref, kg_ref, q_ref, k_ref):
    total = a_ref[...] + b_ref[...]
    q_ref[...] = total / qg_ref[...]
    k_ref[...] = total / kg_ref[...]


def small_call(kernel, shapes, name, *args):
    return pl.pallas_call(
        kernel,
        in_specs=[pl.BlockSpec(memory_space=pltpu.VMEM)] * len(args),
        out_specs=[pl.BlockSpec(memory_space=pltpu.VMEM)] * len(shapes),
        out_shape=[jax.ShapeDtypeStruct(shape, jnp.float32) for shape in shapes],
        compiler_params=pltpu.CompilerParams(vmem_limit_bytes=2 << 20),
        name=name,
    )(*args)


def clip_gains(live, back, q_gain, k_gain):
    size = lax.axis_size("clip")
    rows = q_gain.shape[0] // BLK
    total = pl.pallas_call(
        gains_kernel,
        in_specs=[pl.BlockSpec(memory_space=pltpu.SMEM), pl.BlockSpec(memory_space=pltpu.VMEM)],
        out_specs=pl.BlockSpec(memory_space=pltpu.VMEM),
        out_shape=jax.ShapeDtypeStruct((rows, BLK), jnp.float32),
        scratch_shapes=rank_scratch(rows),
        compiler_params=pltpu.CompilerParams(vmem_limit_bytes=2 << 20),
        name="gains",
    )(live, back)
    flips = [1, 2, 6]
    for n, flip in enumerate(flips):
        other = lax.ppermute(total, "clip", [(i, i ^ flip) for i in range(size)])
        if n < len(flips) - 1:
            (total,) = small_call(add_kernel, [(rows, BLK)], "add", total, other)
    q, k = small_call(
        last_kernel,
        [(rows, BLK)] * 2,
        "last",
        total,
        other,
        q_gain.reshape(rows, BLK),
        k_gain.reshape(rows, BLK),
    )
    return q.reshape(-1), k.reshape(-1)


def shards(query_raw, key_raw, value, upstream, query_gain, key_gain, key_blocks, live):
    groups = lax.axis_size("seq")
    heads = key_blocks.shape[1] // groups
    mine = lax.axis_index("seq").reshape(1)
    lists = jnp.transpose(key_blocks[0], (1, 2, 0))
    packed = pack(
        live, query_raw[0], key_raw[0], value[0], upstream[0], query_gain, key_gain, groups, heads
    )
    packed, mine = lax.optimization_barrier((packed, mine))
    arrived = lax.all_to_all(packed, "seq", split_axis=0, concat_axis=0, tiled=True)
    results = attention(mine, lists, live, arrived, heads)
    back = lax.all_to_all(results, "seq", split_axis=0, concat_axis=0, tiled=True)
    attended, grad_query, grad_key, grad_value = unpack(
        live, back, query_raw[0], key_raw[0], query_gain, key_gain
    )
    q_total, k_total = clip_gains(live, back, query_gain, key_gain)
    return (
        attended[None],
        grad_query[None],
        grad_key[None],
        grad_value[None],
        q_total,
        k_total,
    )


def solution(mesh):
    tokens = P("clip", "seq", None)
    return jax.shard_map(
        shards,
        mesh=mesh,
        in_specs=(tokens,) * 4 + (P(), P(), P("clip", None, None, None), P("clip", None)),
        out_specs=(tokens,) * 4 + (P(), P()),
        check_vma=False,
    )
```

```python
import jax
import jax.numpy as jnp
from jax import lax
from jax.experimental import pallas as pl
from jax.experimental.pallas import tpu as pltpu
from jax.sharding import PartitionSpec as P

BLK = 128
EPSILON = 1e-06
ROWS = 64
CHUNKS = 2
PARTS = 3
SPARE = 8
PLACE, ORDER = range(2)
QUERY, COTANGENT, KEY, VALUE = range(4)
GRAD_Q, OUT, GRAD_K, GRAD_V = range(4)
LOG2E = 1.4426950408889634


def contract(a, b, dims):
    return lax.dot_general(a, b, (dims, ((), ())), preferred_element_type=jnp.float32)


def inverse_rms(x):
    return lax.rsqrt(jnp.mean(x * x, axis=-1, keepdims=True) + EPSILON)


def rank_heads(live_ref, table_ref):
    count = table_ref.shape[1]
    most = lax.fori_loop(0, count, lambda h, n: n + (live_ref[0, h] >= 4).astype(jnp.int32), 0)
    some = lax.fori_loop(0, count, lambda h, n: n + (live_ref[0, h] >= 3).astype(jnp.int32), 0)

    def put(h, counts):
        four, three, two = counts
        is_four = live_ref[0, h] >= 4
        is_three = jnp.logical_and(live_ref[0, h] >= 3, jnp.logical_not(is_four))
        rank = jnp.where(is_four, four, jnp.where(is_three, three, two))
        table_ref[PLACE, h] = rank
        table_ref[ORDER, rank] = h
        step = jnp.logical_not(jnp.logical_or(is_four, is_three))
        return (
            four + is_four.astype(jnp.int32),
            three + is_three.astype(jnp.int32),
            two + step.astype(jnp.int32),
        )

    lax.fori_loop(0, count, put, (jnp.int32(0), most, some))


def group_and_slot(rank, groups):
    second = rank >= groups
    return jnp.where(second, 2 * groups - 1 - rank, rank), second.astype(jnp.int32)


def pack_kernel(
    live_hbm,
    q_hbm,
    k_hbm,
    v_hbm,
    u_hbm,
    qg_hbm,
    kg_hbm,
    out_ref,
    table_ref,
    raw_ref,
    gain_ref,
    live_ref,
    raw_sems,
    gain_sems,
    copy_sems,
    live_sem,
):
    groups, span, both = out_ref.shape
    width = both // 2
    tokens = raw_ref.shape[1]
    heads = span // (2 * tokens)
    step = tokens // CHUNKS

    loads = [
        [
            pltpu.make_async_copy(
                hbm.at[pl.ds(c * step, step)],
                raw_ref.at[n, pl.ds(c * step, step)],
                raw_sems.at[n, c],
            )
            for c in range(CHUNKS)
        ]
        for n, hbm in enumerate((q_hbm, k_hbm))
    ]
    gain_loads = [
        pltpu.make_async_copy(hbm, gain_ref.at[n], gain_sems.at[n])
        for n, hbm in enumerate((qg_hbm, kg_hbm))
    ]
    live_load = pltpu.make_async_copy(live_hbm, live_ref, live_sem)
    live_load.start()
    for n in range(2):
        gain_loads[n].start()
        loads[n][0].start()
    for c in range(1, CHUNKS):
        for n in range(2):
            loads[n][c].start()
    live_load.wait()
    rank_heads(live_ref, table_ref)
    moves, spots = [], []
    for head in range(groups * heads):
        group, slot = group_and_slot(table_ref[PLACE, head], groups)
        spots.append((group, slot))
        for n, (hbm, pair) in enumerate(((u_hbm, 0), (v_hbm, 1))):
            first = pl.multiple_of((pair * heads + slot) * tokens, tokens)
            moves.append(
                pltpu.make_async_copy(
                    hbm.at[:, pl.ds(head * width, width)],
                    out_ref.at[group, pl.ds(first, tokens), pl.ds(width, width)],
                    copy_sems.at[head, n],
                )
            )
    for move in moves:
        move.start()
    for c in range(CHUNKS):
        for n in range(2):
            if c == 0:
                gain_loads[n].wait()
            loads[n][c].wait()

            def some_rows(i, carry):
                row = pl.multiple_of(c * step + i * ROWS, ROWS)
                x = raw_ref[n, pl.ds(row, ROWS)].astype(jnp.float32)
                y = (x * inverse_rms(x) * gain_ref[n]).astype(jnp.bfloat16)
                for head, (group, slot) in enumerate(spots):
                    first = pl.multiple_of((n * heads + slot) * tokens + row, ROWS)
                    at = head * width
                    out_ref[group, pl.ds(first, ROWS), :width] = y[:, at : at + width]
                return carry

            lax.fori_loop(0, step // ROWS, some_rows, 0)
    for move in moves:
        move.wait()


def in_hbm(x):
    return pltpu.with_memory_space_constraint(x, pltpu.HBM)


def pack(live, q, k, v, u, q_gain, k_gain, groups, heads):
    tokens, features = q.shape
    width = features // (groups * heads)
    hbm = pl.BlockSpec(memory_space=pltpu.HBM)
    vmem = pl.BlockSpec(memory_space=pltpu.VMEM)
    return pl.pallas_call(
        pack_kernel,
        in_specs=[hbm] * 7,
        out_specs=[vmem, pl.BlockSpec(memory_space=pltpu.SMEM)],
        out_shape=[
            jax.ShapeDtypeStruct((groups, 2 * heads * tokens, 2 * width), jnp.bfloat16),
            jax.ShapeDtypeStruct((2, groups * heads), jnp.int32),
        ],
        scratch_shapes=[
            pltpu.VMEM((2, tokens, features), jnp.bfloat16),
            pltpu.VMEM((2, 1, features), jnp.float32),
            pltpu.SMEM(live.shape, jnp.int32),
            pltpu.SemaphoreType.DMA((2, CHUNKS)),
            pltpu.SemaphoreType.DMA((2,)),
            pltpu.SemaphoreType.DMA((groups * heads, 2)),
            pltpu.SemaphoreType.DMA(()),
        ],
        compiler_params=pltpu.CompilerParams(vmem_limit_bytes=12 << 20),
        name="pack",
    )(*(in_hbm(x) for x in (live, q, k, v, u, q_gain[None], k_gain[None])))


def attention_kernel(mine_ref, table_ref, lists_ref, live_ref, in_ref, out_ref, *scratch):
    blocks, span, both = in_ref.shape
    heads = len(scratch) // 3
    width = both // 2
    scale = width ** (-0.5)
    turned, sums, ahead, gains_ref = scratch[:heads], scratch[heads : 2 * heads], scratch[2 * heads : -1], scratch[-1]
    mine = mine_ref[0]
    owned = [table_ref[ORDER, rank] for rank in (mine, 2 * blocks - 1 - mine)]
    live = [live_ref[0, h] for h in owned]

    def place(pair, head):
        return pl.ds((pair * heads + head) * BLK, BLK)

    def parts(row):
        pieces = []
        for _ in range(PARTS):
            pieces.append(row.astype(jnp.bfloat16))
            row = row - pieces[-1].astype(jnp.float32)
        return pieces

    def prepare(j, carry):
        for head in range(heads):
            turned[head][j] = in_ref[j, place(1, head)].T
            sums[head][j] = jnp.zeros((BLK, both), jnp.float32)
        return carry

    lax.fori_loop(0, blocks, prepare, 0, unroll=4)

    def start(b, head, slots):
        q = in_ref[b, place(0, head), :width]
        u = in_ref[b, place(0, head), width:]
        diagonal = (q, u)
        chosen = [lists_ref[b, s, owned[head]] for s in range(slots)]
        rows = jnp.concatenate([in_ref[j, place(1, head)] for j in chosen], axis=0)
        scores = contract(rows[:, :width], q, ((1,), (1,)))
        grads = contract(rows[:, width:], u, ((1,), (1,)))
        products = ([scores[s * BLK : (s + 1) * BLK] for s in range(slots)], [grads[s * BLK : (s + 1) * BLK] for s in range(slots)])
        return q, diagonal, chosen, products

    def softmax(products):
        scores, grads = products
        factor = scale * LOG2E
        tops = [jnp.max(s, axis=0, keepdims=True) * factor for s in scores]
        top = tops[0]
        for t in tops[1:]:
            top = jnp.maximum(top, t)
        raised = [jnp.exp2(s * factor - top) for s in scores]
        total = raised[0]
        inner = raised[0] * grads[0]
        for e, g in zip(raised[1:], grads[1:]):
            total = total + e
            inner = inner + e * g
        inverse = 1.0 / jnp.sum(total, axis=0, keepdims=True)
        delta = jnp.sum(inner, axis=0, keepdims=True) * inverse
        probs = [e * inverse for e in raised]
        low = [p.astype(jnp.bfloat16) for p in probs]
        ds = [(p * ((g - delta) * scale)).astype(jnp.bfloat16) for p, g in zip(probs, grads)]
        return low, ds

    def finish_block(b, head, q, diagonal, chosen, low, ds):
        keys = jnp.concatenate([turned[head][j, :width] for j in chosen], axis=1)
        values = jnp.concatenate([turned[head][j, width:] for j in chosen], axis=1)
        out_t = contract(values, jnp.concatenate(low, axis=0), ((1,), (0,)))
        dq_t = contract(keys, jnp.concatenate(ds, axis=0), ((1,), (0,)))
        q, u = diagonal
        more_k = contract(jnp.concatenate(ds, axis=0), q, ((1,), (0,)))
        more_v = contract(jnp.concatenate(low, axis=0), u, ((1,), (0,)))
        old = [sums[head][j] for j in chosen]
        for s, (j, o) in enumerate(zip(chosen, old)):
            sums[head][j, :, :width] = o[:, :width] + more_k[s * BLK : (s + 1) * BLK]
            sums[head][j, :, width:] = o[:, width:] + more_v[s * BLK : (s + 1) * BLK]
        dq = dq_t.astype(jnp.bfloat16).T
        out_ref[b, place(0, head), :width] = dq
        out_ref[b, place(0, head), width:] = out_t.astype(jnp.bfloat16).T
        return jnp.sum(dq.astype(jnp.float32) * q.astype(jnp.float32), axis=0, keepdims=True)

    for slots in ((2, 2), (3, 2), (3, 3), (4, 2), (4, 3), (4, 4)):

        @pl.when(jnp.logical_and(live[0] == slots[0], live[1] == slots[1]))
        def _():
            def keep(h, products):
                for s in range(slots[h]):
                    for n in range(2):
                        ahead[h][n, s] = products[n][s]

            def step(b, gain):
                done = []
                for h in range(heads):
                    products = [[ahead[h][n, s] for s in range(slots[h])] for n in range(2)]
                    after = h + 1 if h + 1 < heads else 0
                    at = b if h + 1 < heads else jnp.minimum(b + 1, blocks - 1)
                    keep(after, start(at, after, slots[after])[3])
                    low, ds = softmax(products)
                    q = in_ref[b, place(0, h), :width]
                    u = in_ref[b, place(0, h), width:]
                    chosen = [lists_ref[b, s, owned[h]] for s in range(slots[h])]
                    done.append(gain[h] + finish_block(b, h, q, (q, u), chosen, low, ds))
                return tuple(done)

            keep(0, start(0, 0, slots[0])[3])

            gain = lax.fori_loop(
                0, blocks, step, (jnp.zeros((1, width), jnp.float32),) * heads, unroll=4
            )
            for h in range(heads):
                gains_ref[h : h + 1] = gain[h]

    extra = parts(jnp.concatenate([gains_ref[h : h + 1] for h in range(heads)], axis=1))
    extra.append(jnp.zeros((SPARE - PARTS, both), jnp.bfloat16))
    extra = jnp.concatenate(extra, axis=0)

    def finish(j, carry):
        for head in range(heads):
            out_ref[j, place(1, head)] = sums[head][j].astype(jnp.bfloat16)
        out_ref[j, span:] = extra
        return carry

    lax.fori_loop(0, blocks, finish, 0, unroll=4)


def attention(mine, table, lists, live, arrived, heads):
    blocks, span, both = arrived.shape
    vmem = pl.BlockSpec(memory_space=pltpu.VMEM)
    smem = pl.BlockSpec(memory_space=pltpu.SMEM)
    return pl.pallas_call(
        attention_kernel,
        in_specs=[smem, smem, smem, smem, vmem],
        out_specs=vmem,
        out_shape=jax.ShapeDtypeStruct((blocks, span + SPARE, both), jnp.bfloat16),
        scratch_shapes=[pltpu.VMEM((blocks, both, BLK), jnp.bfloat16)] * heads
        + [pltpu.VMEM((blocks, BLK, both), jnp.float32)] * heads
        + [pltpu.VMEM((2, lists.shape[1], BLK, BLK), jnp.float32)] * heads
        + [pltpu.VMEM((heads, both // 2), jnp.float32)],
        compiler_params=pltpu.CompilerParams(vmem_limit_bytes=24 << 20),
        name="attention",
    )(mine, table, lists, live, arrived)


def unpack_kernel(
    table_ref,
    back_ref,
    q_ref,
    k_ref,
    qg_ref,
    kg_ref,
    out_hbm,
    dq_hbm,
    dk_hbm,
    dv_hbm,
    done_ref,
    sems,
    copy_sems,
):
    groups, _, both = back_ref.shape
    width = both // 2
    tokens, features = q_ref.shape
    heads = features // (groups * width)
    step = tokens // CHUNKS
    moves, spots = [], []
    for head in range(groups * heads):
        group, slot = group_and_slot(table_ref[PLACE, head], groups)
        spots.append((group, slot))
        for n, hbm in enumerate((out_hbm, dv_hbm)):
            first = pl.multiple_of((n * heads + slot) * tokens, tokens)
            moves.append(
                pltpu.make_async_copy(
                    back_ref.at[group, pl.ds(first, tokens), pl.ds(width, width)],
                    hbm.at[:, pl.ds(head * width, width)],
                    copy_sems.at[head, n],
                )
            )
    for move in moves:
        move.start()
    for c in range(CHUNKS):
        for n, (raw_ref, gain_ref, hbm) in enumerate(
            ((q_ref, qg_ref, dq_hbm), (k_ref, kg_ref, dk_hbm))
        ):

            def some_rows(i, carry):
                row = pl.multiple_of(c * step + i * ROWS, ROWS)
                x = raw_ref[pl.ds(row, ROWS)].astype(jnp.float32)
                inverse = inverse_rms(x)
                unit = x * inverse
                pieces = []
                for group, slot in spots:
                    first = pl.multiple_of((n * heads + slot) * tokens + row, ROWS)
                    pieces.append(back_ref[group, pl.ds(first, ROWS), :width])
                grads = jnp.concatenate(pieces, axis=-1)
                g = grads.astype(jnp.float32) * gain_ref[...]
                mean = jnp.mean(g * unit, axis=-1, keepdims=True)
                done_ref[n, pl.ds(row, ROWS)] = (inverse * (g - unit * mean)).astype(jnp.bfloat16)
                return carry

            lax.fori_loop(0, step // ROWS, some_rows, 0)
            move = pltpu.make_async_copy(
                done_ref.at[n, pl.ds(c * step, step)], hbm.at[pl.ds(c * step, step)], sems.at[n, c]
            )
            move.start()
            moves.append(move)
    for move in moves:
        move.wait()


def unpack(table, back, q, k, q_gain, k_gain):
    groups, _, both = back.shape
    tokens, features = q.shape
    hbm = pl.BlockSpec(memory_space=pltpu.HBM)
    vmem = pl.BlockSpec(memory_space=pltpu.VMEM)
    return pl.pallas_call(
        unpack_kernel,
        in_specs=[pl.BlockSpec(memory_space=pltpu.SMEM)] + [vmem] * 5,
        out_specs=[hbm] * 4,
        out_shape=[jax.ShapeDtypeStruct((tokens, features), jnp.bfloat16)] * 4,
        scratch_shapes=[
            pltpu.VMEM((2, tokens, features), jnp.bfloat16),
            pltpu.SemaphoreType.DMA((2, CHUNKS)),
            pltpu.SemaphoreType.DMA((2 * features // both, 2)),
        ],
        compiler_params=pltpu.CompilerParams(vmem_limit_bytes=12 << 20),
        name="unpack",
    )(table, back, q, k, q_gain[None], k_gain[None])


def gains_kernel(table_ref, back_ref, out_ref):
    groups, rows, _ = back_ref.shape
    heads, width = out_ref.shape
    for head in range(heads):
        group, slot = group_and_slot(table_ref[PLACE, head], groups)
        extra = back_ref[group, rows - SPARE :].astype(jnp.float32)
        total = extra[0:1]
        for n in range(1, PARTS):
            total = total + extra[n : n + 1]
        out_ref[head : head + 1] = jnp.where(slot == 0, total[:, :width], total[:, width:])


def add_kernel(a_ref, b_ref, out_ref):
    out_ref[...] = a_ref[...] + b_ref[...]


def last_kernel(a_ref, b_ref, qg_ref, kg_ref, q_ref, k_ref):
    total = a_ref[...] + b_ref[...]
    q_ref[...] = total / qg_ref[...]
    k_ref[...] = total / kg_ref[...]


def small_call(kernel, shapes, name, *args):
    return pl.pallas_call(
        kernel,
        in_specs=[pl.BlockSpec(memory_space=pltpu.VMEM)] * len(args),
        out_specs=[pl.BlockSpec(memory_space=pltpu.VMEM)] * len(shapes),
        out_shape=[jax.ShapeDtypeStruct(shape, jnp.float32) for shape in shapes],
        compiler_params=pltpu.CompilerParams(vmem_limit_bytes=2 << 20),
        name=name,
    )(*args)


def clip_gains(table, back, q_gain, k_gain):
    size = lax.axis_size("clip")
    rows = q_gain.shape[0] // BLK
    total = pl.pallas_call(
        gains_kernel,
        in_specs=[pl.BlockSpec(memory_space=pltpu.SMEM), pl.BlockSpec(memory_space=pltpu.VMEM)],
        out_specs=pl.BlockSpec(memory_space=pltpu.VMEM),
        out_shape=jax.ShapeDtypeStruct((rows, BLK), jnp.float32),
        compiler_params=pltpu.CompilerParams(vmem_limit_bytes=2 << 20),
        name="gains",
    )(table, back)
    flips = [1, 2, 6]
    for n, flip in enumerate(flips):
        other = lax.ppermute(total, "clip", [(i, i ^ flip) for i in range(size)])
        if n < len(flips) - 1:
            (total,) = small_call(add_kernel, [(rows, BLK)], "add", total, other)
    q, k = small_call(
        last_kernel,
        [(rows, BLK)] * 2,
        "last",
        total,
        other,
        q_gain.reshape(rows, BLK),
        k_gain.reshape(rows, BLK),
    )
    return q.reshape(-1), k.reshape(-1)


def shards(query_raw, key_raw, value, upstream, query_gain, key_gain, key_blocks, live):
    groups = lax.axis_size("seq")
    heads = key_blocks.shape[1] // groups
    mine = lax.axis_index("seq").reshape(1)
    lists = jnp.transpose(key_blocks[0], (1, 2, 0))
    packed, table = pack(
        live, query_raw[0], key_raw[0], value[0], upstream[0], query_gain, key_gain, groups, heads
    )
    packed, mine = lax.optimization_barrier((packed, mine))
    arrived = lax.all_to_all(packed, "seq", split_axis=0, concat_axis=0, tiled=True)
    results = attention(mine, table, lists, live, arrived, heads)
    back = lax.all_to_all(results, "seq", split_axis=0, concat_axis=0, tiled=True)
    attended, grad_query, grad_key, grad_value = unpack(
        table, back, query_raw[0], key_raw[0], query_gain, key_gain
    )
    q_total, k_total = clip_gains(table, back, query_gain, key_gain)
    return (
        attended[None],
        grad_query[None],
        grad_key[None],
        grad_value[None],
        q_total,
        k_total,
    )


def solution(mesh):
    tokens = P("clip", "seq", None)
    return jax.shard_map(
        shards,
        mesh=mesh,
        in_specs=(tokens,) * 4 + (P(), P(), P("clip", None, None, None), P("clip", None)),
        out_specs=(tokens,) * 4 + (P(), P()),
        check_vma=False,
    )
```

```python
import jax
import jax.numpy as jnp
from jax import lax
from jax.experimental import pallas as pl
from jax.experimental.pallas import tpu as pltpu
from jax.sharding import PartitionSpec as P

BLK = 128
EPSILON = 1e-06
ROWS = 64
CHUNKS = 2
PARTS = 3
SPARE = 8
UNROLL = 4
QUERY, COTANGENT, KEY, VALUE = range(4)
GRAD_Q, OUT, GRAD_K, GRAD_V = range(4)
LOG2E = 1.4426950408889634


def contract(a, b, dims):
    return lax.dot_general(a, b, (dims, ((), ())), preferred_element_type=jnp.float32)


def inverse_rms(x):
    return lax.rsqrt(jnp.mean(x * x, axis=-1, keepdims=True) + EPSILON)


def pack_kernel(
    q_hbm, k_hbm, v_hbm, u_hbm, qg_hbm, kg_hbm, out_ref, raw_ref, gain_ref, raw_sems, gain_sems, copy_sems
):
    groups, span, both = out_ref.shape
    width = both // 2
    tokens = raw_ref.shape[1]
    heads = span // (2 * tokens)
    step = tokens // CHUNKS

    loads = [
        [
            pltpu.make_async_copy(
                hbm.at[pl.ds(c * step, step)],
                raw_ref.at[n, pl.ds(c * step, step)],
                raw_sems.at[n, c],
            )
            for c in range(CHUNKS)
        ]
        for n, hbm in enumerate((q_hbm, k_hbm))
    ]
    gain_loads = [
        pltpu.make_async_copy(hbm, gain_ref.at[n], gain_sems.at[n])
        for n, hbm in enumerate((qg_hbm, kg_hbm))
    ]
    for n in range(2):
        gain_loads[n].start()
        loads[n][0].start()
    for c in range(1, CHUNKS):
        for n in range(2):
            loads[n][c].start()
    moves = []
    for group in range(groups):
        for head in range(heads):
            at = (group * heads + head) * width
            for n, (hbm, pair) in enumerate(((u_hbm, 0), (v_hbm, 1))):
                first = (pair * heads + head) * tokens
                moves.append(
                    pltpu.make_async_copy(
                        hbm.at[:, pl.ds(at, width)],
                        out_ref.at[group, pl.ds(first, tokens), pl.ds(width, width)],
                        copy_sems.at[group * heads + head, n],
                    )
                )
    for move in moves:
        move.start()
    for c in range(CHUNKS):
        for n in range(2):
            if c == 0:
                gain_loads[n].wait()
            loads[n][c].wait()

            def some_rows(i, carry):
                row = pl.multiple_of(c * step + i * ROWS, ROWS)
                x = raw_ref[n, pl.ds(row, ROWS)].astype(jnp.float32)
                y = (x * inverse_rms(x) * gain_ref[n]).astype(jnp.bfloat16)
                for group in range(groups):
                    for head in range(heads):
                        at = (group * heads + head) * width
                        first = (n * heads + head) * tokens
                        out_ref[group, pl.ds(first + row, ROWS), :width] = y[:, at : at + width]
                return carry

            lax.fori_loop(0, step // ROWS, some_rows, 0)
    for move in moves:
        move.wait()


def in_hbm(x):
    return pltpu.with_memory_space_constraint(x, pltpu.HBM)


def pack(q, k, v, u, q_gain, k_gain, groups, heads):
    tokens, features = q.shape
    width = features // (groups * heads)
    hbm = pl.BlockSpec(memory_space=pltpu.HBM)
    vmem = pl.BlockSpec(memory_space=pltpu.VMEM)
    return pl.pallas_call(
        pack_kernel,
        in_specs=[hbm] * 6,
        out_specs=vmem,
        out_shape=jax.ShapeDtypeStruct((groups, 2 * heads * tokens, 2 * width), jnp.bfloat16),
        scratch_shapes=[
            pltpu.VMEM((2, tokens, features), jnp.bfloat16),
            pltpu.VMEM((2, 1, features), jnp.float32),
            pltpu.SemaphoreType.DMA((2, CHUNKS)),
            pltpu.SemaphoreType.DMA((2,)),
            pltpu.SemaphoreType.DMA((groups * heads, 2)),
        ],
        compiler_params=pltpu.CompilerParams(vmem_limit_bytes=12 << 20),
        name="pack",
    )(*(in_hbm(x) for x in (q, k, v, u, q_gain[None], k_gain[None])))


def head_pass(owner, lists_ref, live_ref, source, put_query, put_key, scratch, after_step, after_keys):
    turned_ref, sums_ref, ahead_ref, sum_ref = scratch
    blocks, both, _ = turned_ref.shape
    width = both // 2
    scale = width ** (-0.5)
    query_rows, key_rows = source

    def prepare(j, carry):
        turned_ref[j] = key_rows(j).T
        sums_ref[j] = jnp.zeros((BLK, both), jnp.float32)
        return carry

    lax.fori_loop(0, blocks, prepare, 0, unroll=4)

    def softmax(scores, grads):
        factor = scale * LOG2E
        top = scores[0]
        for s in scores[1:]:
            top = jnp.maximum(top, s)
        top = jnp.max(top, axis=0, keepdims=True) * factor
        raised = [jnp.exp2(s * factor - top) for s in scores]
        total = raised[0]
        inner = raised[0] * grads[0]
        for e, g in zip(raised[1:], grads[1:]):
            total = total + e
            inner = inner + e * g
        inverse = 1.0 / jnp.sum(total, axis=0, keepdims=True)
        delta = jnp.sum(inner, axis=0, keepdims=True) * inverse
        probs = [e * inverse for e in raised]
        low = [p.astype(jnp.bfloat16) for p in probs]
        ds = [(p * ((g - delta) * scale)).astype(jnp.bfloat16) for p, g in zip(probs, grads)]
        return low, ds

    def finish_block(b, slots, low, ds):
        rows = query_rows(b)
        q, u = rows[:, :width], rows[:, width:]
        chosen = [lists_ref[b, s, owner] for s in range(slots)]
        keys = jnp.concatenate([turned_ref[j, :width] for j in chosen], axis=1)
        values = jnp.concatenate([turned_ref[j, width:] for j in chosen], axis=1)
        ds_all = jnp.concatenate(ds, axis=0)
        low_all = jnp.concatenate(low, axis=0)
        out_t = contract(values, low_all, ((1,), (0,)))
        dq_t = contract(keys, ds_all, ((1,), (0,)))
        more_k = contract(ds_all, q, ((1,), (0,)))
        more_v = contract(low_all, u, ((1,), (0,)))
        old = [sums_ref[j] for j in chosen]
        for s, (j, o) in enumerate(zip(chosen, old)):
            sums_ref[j, :, :width] = o[:, :width] + more_k[s * BLK : (s + 1) * BLK]
            sums_ref[j, :, width:] = o[:, width:] + more_v[s * BLK : (s + 1) * BLK]
        dq = dq_t.astype(jnp.bfloat16).T
        put_query(b, dq, out_t.astype(jnp.bfloat16).T)
        return jnp.sum(dq.astype(jnp.float32) * q.astype(jnp.float32), axis=0, keepdims=True)

    for slots in (2, 3, 4):

        @pl.when(live_ref[0, owner] == slots)
        def _():
            def step(i, gain):
                for k in range(UNROLL):
                    b = UNROLL * i + k
                    scores, grads = [
                        [ahead_ref[k % 2, n, s] for s in range(slots)] for n in range(2)
                    ]
                    start_at(b + 1, (k + 1) % 2, slots)
                    low, ds = softmax(scores, grads)
                    gain = gain + finish_block(b, slots, low, ds)
                after_step(i)
                return gain

            def start_at(b, side, slots):
                b = jnp.minimum(b, blocks - 1)
                rows = query_rows(b)
                keys = jnp.concatenate(
                    [key_rows(lists_ref[b, s, owner]) for s in range(slots)], axis=0
                )
                scores = contract(keys[:, :width], rows[:, :width], ((1,), (1,)))
                grads = contract(keys[:, width:], rows[:, width:], ((1,), (1,)))
                for s in range(slots):
                    ahead_ref[side, 0, s] = scores[s * BLK : (s + 1) * BLK]
                    ahead_ref[side, 1, s] = grads[s * BLK : (s + 1) * BLK]

            start_at(0, 0, slots)
            sum_ref[...] = lax.fori_loop(
                0, blocks // UNROLL, step, jnp.zeros((1, width), jnp.float32)
            )

    def finish(i, carry):
        for k in range(UNROLL):
            j = UNROLL * i + k
            put_key(j, sums_ref[j].astype(jnp.bfloat16))
        after_keys(i)
        return carry

    lax.fori_loop(0, blocks // UNROLL, finish, 0)


def first_head_kernel(
    mine_ref, lists_ref, live_ref, in_ref, out_hbm, rest_hbm, keys_hbm, sum_ref, *scratch
):
    *scratch, out_ref, keys_ref, sems, out_sems, keys_sems = scratch
    moves = [
        pltpu.make_async_copy(
            in_ref.at[:, pl.ds(source * BLK, BLK)], rest_hbm.at[:, pl.ds(n * BLK, BLK)], sems.at[n]
        )
        for n, source in enumerate((1, 3))
    ]
    for move in moves:
        move.start()

    def put_query(b, dq, out):
        width = dq.shape[1]
        out_ref[b, :, :width] = dq
        out_ref[b, :, width:] = out

    def put_key(j, grads):
        keys_ref[j] = grads

    def store(i, ref, hbm, sems):
        at = pl.multiple_of(i * UNROLL, UNROLL)
        return pltpu.make_async_copy(ref.at[pl.ds(at, UNROLL)], hbm.at[pl.ds(at, UNROLL)], sems.at[i])

    source = (lambda b: in_ref[b, :BLK], lambda j: in_ref[j, 2 * BLK : 3 * BLK])
    head_pass(
        2 * mine_ref[0],
        lists_ref,
        live_ref,
        source,
        put_query,
        put_key,
        (*scratch, sum_ref),
        lambda i: store(i, out_ref, out_hbm, out_sems).start(),
        lambda i: store(i, keys_ref, keys_hbm, keys_sems).start(),
    )
    for i in range(in_ref.shape[0] // UNROLL):
        store(i, out_ref, out_hbm, out_sems).wait()
        store(i, keys_ref, keys_hbm, keys_sems).wait()
    for move in moves:
        move.wait()


def second_head_kernel(
    mine_ref, lists_ref, live_ref, in_ref, keys_hbm, before_ref, out_ref, sums_ref, *scratch
):
    *scratch, sum_ref, sems = scratch
    move = pltpu.make_async_copy(keys_hbm, out_ref.at[:, pl.ds(0, BLK)], sems.at[0])
    move.start()

    def put_query(b, dq, out):
        width = dq.shape[1]
        out_ref[b, BLK : 2 * BLK, :width] = dq
        out_ref[b, BLK : 2 * BLK, width:] = out

    def put_key(j, grads):
        out_ref[j, 2 * BLK : 3 * BLK] = grads

    source = (lambda b: in_ref[b, :BLK], lambda j: in_ref[j, BLK : 2 * BLK])
    head_pass(
        2 * mine_ref[0] + 1,
        lists_ref,
        live_ref,
        source,
        put_query,
        put_key,
        (*scratch, sum_ref),
        lambda i: None,
        lambda i: None,
    )
    sums_ref[0:1] = before_ref[...]
    sums_ref[1:2] = sum_ref[...]
    move.wait()


def head_scratch(blocks, both, slots):
    return [
        pltpu.VMEM((blocks, both, BLK), jnp.bfloat16),
        pltpu.VMEM((blocks, BLK, both), jnp.float32),
        pltpu.VMEM((2, 2, slots, BLK, BLK), jnp.float32),
    ]


def first_head(mine, lists, live, arrived):
    blocks, _, both = arrived.shape
    vmem = pl.BlockSpec(memory_space=pltpu.VMEM)
    smem = pl.BlockSpec(memory_space=pltpu.SMEM)
    hbm = pl.BlockSpec(memory_space=pltpu.HBM)
    return pl.pallas_call(
        first_head_kernel,
        in_specs=[smem, smem, smem, vmem],
        out_specs=[hbm, hbm, hbm, vmem],
        out_shape=[
            pltpu.HBM((blocks, BLK, both), jnp.bfloat16),
            pltpu.HBM((blocks, 2 * BLK, both), jnp.bfloat16),
            pltpu.HBM((blocks, BLK, both), jnp.bfloat16),
            jax.ShapeDtypeStruct((1, both // 2), jnp.float32),
        ],
        scratch_shapes=head_scratch(blocks, both, lists.shape[1])
        + [
            pltpu.VMEM((blocks, BLK, both), jnp.bfloat16),
            pltpu.VMEM((blocks, BLK, both), jnp.bfloat16),
            pltpu.SemaphoreType.DMA((2,)),
            pltpu.SemaphoreType.DMA((blocks // UNROLL,)),
            pltpu.SemaphoreType.DMA((blocks // UNROLL,)),
        ],
        compiler_params=pltpu.CompilerParams(vmem_limit_bytes=20 << 20),
        name="first_head",
    )(mine, lists, live, arrived)


def second_head(mine, lists, live, rest, keys, before):
    blocks, _, both = rest.shape
    vmem = pl.BlockSpec(memory_space=pltpu.VMEM)
    smem = pl.BlockSpec(memory_space=pltpu.SMEM)
    return pl.pallas_call(
        second_head_kernel,
        in_specs=[smem, smem, smem, vmem, pl.BlockSpec(memory_space=pltpu.HBM), vmem],
        out_specs=[vmem] * 2,
        out_shape=[
            jax.ShapeDtypeStruct((blocks, 3 * BLK + SPARE, both), jnp.bfloat16),
            jax.ShapeDtypeStruct((2, both // 2), jnp.float32),
        ],
        scratch_shapes=head_scratch(blocks, both, lists.shape[1])
        + [pltpu.VMEM((1, both // 2), jnp.float32), pltpu.SemaphoreType.DMA((1,))],
        compiler_params=pltpu.CompilerParams(vmem_limit_bytes=20 << 20),
        name="second_head",
    )(mine, lists, live, rest, in_hbm(keys), before)


def add_kernel(a_ref, b_ref, out_ref):
    out_ref[...] = a_ref[...] + b_ref[...]


def add(a, b):
    vmem = pl.BlockSpec(memory_space=pltpu.VMEM)
    return pl.pallas_call(
        add_kernel,
        in_specs=[vmem] * 2,
        out_specs=vmem,
        out_shape=jax.ShapeDtypeStruct(a.shape, a.dtype),
        compiler_params=pltpu.CompilerParams(vmem_limit_bytes=1 << 20),
        name="add",
    )(a, b)


def attach_kernel(a_ref, b_ref, given_ref, out_ref, extra_ref, sems):
    del given_ref
    total = a_ref[...] + b_ref[...]
    row = jnp.concatenate([total[n : n + 1] for n in range(total.shape[0])], axis=1)
    pieces = []
    for _ in range(PARTS):
        pieces.append(row.astype(jnp.bfloat16))
        row = row - pieces[-1].astype(jnp.float32)
    pieces.append(jnp.zeros((SPARE - PARTS, row.shape[1]), jnp.bfloat16))
    extra_ref[...] = jnp.concatenate(pieces, axis=0)
    moves = [
        pltpu.make_async_copy(extra_ref, out_ref.at[j, pl.ds(3 * BLK, SPARE)], sems.at[j])
        for j in range(out_ref.shape[0])
    ]
    for move in moves:
        move.start()
    for move in moves:
        move.wait()


def attach(a, b, results):
    vmem = pl.BlockSpec(memory_space=pltpu.VMEM)
    anywhere = pl.BlockSpec(memory_space=pl.ANY)
    return pl.pallas_call(
        attach_kernel,
        in_specs=[vmem, vmem, anywhere],
        out_specs=anywhere,
        out_shape=jax.ShapeDtypeStruct(results.shape, results.dtype),
        scratch_shapes=[
            pltpu.VMEM((SPARE, results.shape[2]), results.dtype),
            pltpu.SemaphoreType.DMA((results.shape[0],)),
        ],
        input_output_aliases={2: 0},
        compiler_params=pltpu.CompilerParams(vmem_limit_bytes=1 << 20),
        name="attach",
    )(a, b, results)


def unpack_kernel(
    first_ref,
    back_ref,
    q_ref,
    k_ref,
    qg_ref,
    kg_ref,
    qr_ref,
    kr_ref,
    out_hbm,
    dq_hbm,
    dk_hbm,
    dv_hbm,
    q_total_ref,
    k_total_ref,
    done_ref,
    sems,
    copy_sems,
):
    groups, _, both = back_ref.shape
    width = both // 2
    tokens, features = q_ref.shape
    step = tokens // CHUNKS
    places = (((first_ref, 0), (back_ref, tokens)), ((back_ref, 0), (back_ref, 2 * tokens)))
    moves = []
    for group in range(groups):
        for head in range(2):
            at = (2 * group + head) * width
            for n, hbm in enumerate((out_hbm, dv_hbm)):
                ref, row = places[n][head]
                moves.append(
                    pltpu.make_async_copy(
                        ref.at[group, pl.ds(row, tokens), pl.ds(width, width)],
                        hbm.at[:, pl.ds(at, width)],
                        copy_sems.at[2 * group + head, n],
                    )
                )
    for move in moves:
        move.start()
    for c in range(CHUNKS):
        for n, (raw_ref, gain_ref, hbm) in enumerate(
            ((q_ref, qg_ref, dq_hbm), (k_ref, kg_ref, dk_hbm))
        ):

            def some_rows(i, carry):
                row = pl.multiple_of(c * step + i * ROWS, ROWS)
                x = raw_ref[pl.ds(row, ROWS)].astype(jnp.float32)
                inverse = inverse_rms(x)
                unit = x * inverse
                pieces = []
                for group in range(groups):
                    for ref, first in places[n]:
                        pieces.append(ref[group, pl.ds(first + row, ROWS), :width])
                g = jnp.concatenate(pieces, axis=-1).astype(jnp.float32) * gain_ref[...]
                mean = jnp.mean(g * unit, axis=-1, keepdims=True)
                done_ref[n, pl.ds(row, ROWS)] = (inverse * (g - unit * mean)).astype(jnp.bfloat16)
                return carry

            lax.fori_loop(0, step // ROWS, some_rows, 0)
            move = pltpu.make_async_copy(
                done_ref.at[n, pl.ds(c * step, step)], hbm.at[pl.ds(c * step, step)], sems.at[n, c]
            )
            move.start()
            moves.append(move)
    rows = []
    for group in range(groups):
        extra = back_ref[group, 3 * tokens :].astype(jnp.float32)
        total = extra[0:1]
        for n in range(1, PARTS):
            total = total + extra[n : n + 1]
        rows += [total[:, :width], total[:, width:]]
    total = jnp.concatenate(rows, axis=0)
    q_total_ref[...] = total / qr_ref[...]
    k_total_ref[...] = total / kr_ref[...]
    for move in moves:
        move.wait()


def unpack(first, back, q, k, q_gain, k_gain):
    tokens, features = q.shape
    hbm = pl.BlockSpec(memory_space=pltpu.HBM)
    vmem = pl.BlockSpec(memory_space=pltpu.VMEM)
    rows = features // BLK
    results = pl.pallas_call(
        unpack_kernel,
        in_specs=[vmem] * 8,
        out_specs=[hbm] * 4 + [vmem] * 2,
        out_shape=[jax.ShapeDtypeStruct((tokens, features), jnp.bfloat16)] * 4
        + [jax.ShapeDtypeStruct((rows, BLK), jnp.float32)] * 2,
        scratch_shapes=[
            pltpu.VMEM((2, tokens, features), jnp.bfloat16),
            pltpu.SemaphoreType.DMA((2, CHUNKS)),
            pltpu.SemaphoreType.DMA((rows, 2)),
        ],
        compiler_params=pltpu.CompilerParams(vmem_limit_bytes=14 << 20),
        name="unpack",
    )(
        first,
        back,
        q,
        k,
        q_gain[None],
        k_gain[None],
        q_gain.reshape(rows, BLK),
        k_gain.reshape(rows, BLK),
    )
    return (*results[:4], results[4].reshape(-1), results[5].reshape(-1))


def shards(query_raw, key_raw, value, upstream, query_gain, key_gain, key_blocks, live):
    groups = lax.axis_size("seq")
    clips = lax.axis_size("clip")
    heads = key_blocks.shape[1] // groups
    mine = lax.axis_index("seq").reshape(1)
    lists = jnp.transpose(key_blocks[0], (1, 2, 0))
    packed = pack(
        query_raw[0], key_raw[0], value[0], upstream[0], query_gain, key_gain, groups, heads
    )
    packed, mine = lax.optimization_barrier((packed, mine))
    arrived = lax.all_to_all(packed, "seq", split_axis=0, concat_axis=0, tiled=True)
    first, rest, keys, before = first_head(mine, lists, live, arrived)
    first_back = lax.all_to_all(first, "seq", split_axis=0, concat_axis=0, tiled=True)
    results, total = second_head(mine, lists, live, rest, keys, before)
    flips = [1, 2, 6]
    for n, flip in enumerate(flips):
        other = lax.ppermute(total, "clip", [(i, i ^ flip) for i in range(clips)])
        if n < len(flips) - 1:
            total = add(total, other)
    results = attach(total, other, results)
    back = lax.all_to_all(results, "seq", split_axis=0, concat_axis=0, tiled=True)
    attended, grad_query, grad_key, grad_value, q_total, k_total = unpack(
        first_back, back, query_raw[0], key_raw[0], query_gain, key_gain
    )
    return (
        attended[None],
        grad_query[None],
        grad_key[None],
        grad_value[None],
        q_total,
        k_total,
    )


def solution(mesh):
    tokens = P("clip", "seq", None)
    return jax.shard_map(
        shards,
        mesh=mesh,
        in_specs=(tokens,) * 4 + (P(), P(), P("clip", None, None, None), P("clip", None)),
        out_specs=(tokens,) * 4 + (P(), P()),
        check_vma=False,
    )
```

```python
import jax
import jax.numpy as jnp
from jax import lax
from jax.experimental import pallas as pl
from jax.experimental.pallas import tpu as pltpu
from jax.sharding import PartitionSpec as P

BLK = 128
EPSILON = 1e-06
ROWS = 64
CHUNKS = 2
PARTS = 3
SPARE = 8
PLACE, ORDER = range(2)
QUERY, COTANGENT, KEY, VALUE = range(4)
GRAD_Q, OUT, GRAD_K, GRAD_V = range(4)
LOG2E = 1.4426950408889634


def contract(a, b, dims):
    return lax.dot_general(a, b, (dims, ((), ())), preferred_element_type=jnp.float32)


def inverse_rms(x):
    return lax.rsqrt(jnp.mean(x * x, axis=-1, keepdims=True) + EPSILON)


def rank_heads(live_ref, table_ref):
    count = table_ref.shape[1]
    lives = [live_ref[0, h] for h in range(count)]
    fours = [(n >= 4).astype(jnp.int32) for n in lives]
    somes = [(n >= 3).astype(jnp.int32) for n in lives]
    four, three, two = jnp.int32(0), sum(fours), sum(somes)
    for h in range(count):
        rank = jnp.where(fours[h] == 1, four, jnp.where(somes[h] == 1, three, two))
        table_ref[PLACE, h] = rank
        table_ref[ORDER, rank] = h
        four = four + fours[h]
        three = three + somes[h] - fours[h]
        two = two + 1 - somes[h]


def group_and_slot(rank, groups):
    second = rank >= groups
    return jnp.where(second, 2 * groups - 1 - rank, rank), second.astype(jnp.int32)


def pack_kernel(
    live_hbm,
    q_hbm,
    k_hbm,
    v_hbm,
    u_hbm,
    qg_hbm,
    kg_hbm,
    out_ref,
    table_ref,
    raw_ref,
    gain_ref,
    live_ref,
    raw_sems,
    gain_sems,
    copy_sems,
    live_sem,
):
    groups, span, both = out_ref.shape
    width = both // 2
    tokens = raw_ref.shape[1]
    heads = span // (2 * tokens)
    step = tokens // CHUNKS

    loads = [
        [
            pltpu.make_async_copy(
                hbm.at[pl.ds(c * step, step)],
                raw_ref.at[n, pl.ds(c * step, step)],
                raw_sems.at[n, c],
            )
            for c in range(CHUNKS)
        ]
        for n, hbm in enumerate((q_hbm, k_hbm))
    ]
    gain_loads = [
        pltpu.make_async_copy(hbm, gain_ref.at[n], gain_sems.at[n])
        for n, hbm in enumerate((qg_hbm, kg_hbm))
    ]
    live_load = pltpu.make_async_copy(live_hbm, live_ref, live_sem)
    live_load.start()
    for n in range(2):
        gain_loads[n].start()
        loads[n][0].start()
    for c in range(1, CHUNKS):
        for n in range(2):
            loads[n][c].start()
    live_load.wait()
    rank_heads(live_ref, table_ref)
    moves, spots = [], []
    for head in range(groups * heads):
        group, slot = group_and_slot(table_ref[PLACE, head], groups)
        spots.append((group, slot))
        for n, (hbm, pair) in enumerate(((u_hbm, 0), (v_hbm, 1))):
            first = pl.multiple_of((pair * heads + slot) * tokens, tokens)
            moves.append(
                pltpu.make_async_copy(
                    hbm.at[:, pl.ds(head * width, width)],
                    out_ref.at[group, pl.ds(first, tokens), pl.ds(width, width)],
                    copy_sems.at[head, n],
                )
            )
    for move in moves:
        move.start()
    for c in range(CHUNKS):
        for n in range(2):
            if c == 0:
                gain_loads[n].wait()
            loads[n][c].wait()

            def some_rows(i, carry):
                row = pl.multiple_of(c * step + i * ROWS, ROWS)
                x = raw_ref[n, pl.ds(row, ROWS)].astype(jnp.float32)
                y = (x * inverse_rms(x) * gain_ref[n]).astype(jnp.bfloat16)
                for head, (group, slot) in enumerate(spots):
                    first = pl.multiple_of((n * heads + slot) * tokens + row, ROWS)
                    at = head * width
                    out_ref[group, pl.ds(first, ROWS), :width] = y[:, at : at + width]
                return carry

            lax.fori_loop(0, step // ROWS, some_rows, 0)
    for move in moves:
        move.wait()


def in_hbm(x):
    return pltpu.with_memory_space_constraint(x, pltpu.HBM)


def pack(live, q, k, v, u, q_gain, k_gain, groups, heads):
    tokens, features = q.shape
    width = features // (groups * heads)
    hbm = pl.BlockSpec(memory_space=pltpu.HBM)
    vmem = pl.BlockSpec(memory_space=pltpu.VMEM)
    return pl.pallas_call(
        pack_kernel,
        in_specs=[hbm] * 7,
        out_specs=[vmem, pl.BlockSpec(memory_space=pltpu.SMEM)],
        out_shape=[
            jax.ShapeDtypeStruct((groups, 2 * heads * tokens, 2 * width), jnp.bfloat16),
            jax.ShapeDtypeStruct((2, groups * heads), jnp.int32),
        ],
        scratch_shapes=[
            pltpu.VMEM((2, tokens, features), jnp.bfloat16),
            pltpu.VMEM((2, 1, features), jnp.float32),
            pltpu.SMEM(live.shape, jnp.int32),
            pltpu.SemaphoreType.DMA((2, CHUNKS)),
            pltpu.SemaphoreType.DMA((2,)),
            pltpu.SemaphoreType.DMA((groups * heads, 2)),
            pltpu.SemaphoreType.DMA(()),
        ],
        compiler_params=pltpu.CompilerParams(vmem_limit_bytes=12 << 20),
        name="pack",
    )(*(in_hbm(x) for x in (live, q, k, v, u, q_gain[None], k_gain[None])))


def attention_kernel(mine_ref, table_ref, live_ref, lists_any, in_ref, out_ref, *scratch):
    *scratch, lists_ref, lists_sem = scratch
    lists_load = pltpu.make_async_copy(lists_any, lists_ref, lists_sem)
    lists_load.start()
    blocks, span, both = in_ref.shape
    heads = len(scratch) // 3
    width = both // 2
    scale = width ** (-0.5)
    turned, sums, ahead, gains_ref = scratch[:heads], scratch[heads : 2 * heads], scratch[2 * heads : -1], scratch[-1]
    mine = mine_ref[0]
    owned = [table_ref[ORDER, rank] for rank in (mine, 2 * blocks - 1 - mine)]
    live = [live_ref[0, h] for h in owned]

    def place(pair, head):
        return pl.ds((pair * heads + head) * BLK, BLK)

    def parts(row):
        pieces = []
        for _ in range(PARTS):
            pieces.append(row.astype(jnp.bfloat16))
            row = row - pieces[-1].astype(jnp.float32)
        return pieces

    def prepare(j, carry):
        for head in range(heads):
            turned[head][j] = in_ref[j, place(1, head)].T
            sums[head][j] = jnp.zeros((BLK, both), jnp.float32)
        return carry

    lax.fori_loop(0, blocks, prepare, 0, unroll=4)
    lists_load.wait()

    def start(b, head, slots):
        q = in_ref[b, place(0, head), :width]
        u = in_ref[b, place(0, head), width:]
        diagonal = (q, u)
        chosen = [lists_ref[b, s, owned[head]] for s in range(slots)]
        rows = jnp.concatenate([in_ref[j, place(1, head)] for j in chosen], axis=0)
        scores = contract(rows[:, :width], q, ((1,), (1,)))
        grads = contract(rows[:, width:], u, ((1,), (1,)))
        products = ([scores[s * BLK : (s + 1) * BLK] for s in range(slots)], [grads[s * BLK : (s + 1) * BLK] for s in range(slots)])
        return q, diagonal, chosen, products

    def softmax(products):
        scores, grads = products
        factor = scale * LOG2E
        tops = [jnp.max(s, axis=0, keepdims=True) * factor for s in scores]
        top = tops[0]
        for t in tops[1:]:
            top = jnp.maximum(top, t)
        raised = [jnp.exp2(s * factor - top) for s in scores]
        total = raised[0]
        inner = raised[0] * grads[0]
        for e, g in zip(raised[1:], grads[1:]):
            total = total + e
            inner = inner + e * g
        inverse = 1.0 / jnp.sum(total, axis=0, keepdims=True)
        delta = jnp.sum(inner, axis=0, keepdims=True) * inverse
        probs = [e * inverse for e in raised]
        low = [p.astype(jnp.bfloat16) for p in probs]
        ds = [(p * ((g - delta) * scale)).astype(jnp.bfloat16) for p, g in zip(probs, grads)]
        return low, ds

    def finish_block(b, head, q, diagonal, chosen, low, ds):
        keys = jnp.concatenate([turned[head][j, :width] for j in chosen], axis=1)
        values = jnp.concatenate([turned[head][j, width:] for j in chosen], axis=1)
        out_t = contract(values, jnp.concatenate(low, axis=0), ((1,), (0,)))
        dq_t = contract(keys, jnp.concatenate(ds, axis=0), ((1,), (0,)))
        q, u = diagonal
        more_k = contract(jnp.concatenate(ds, axis=0), q, ((1,), (0,)))
        more_v = contract(jnp.concatenate(low, axis=0), u, ((1,), (0,)))
        old = [sums[head][j] for j in chosen]
        for s, (j, o) in enumerate(zip(chosen, old)):
            sums[head][j, :, :width] = o[:, :width] + more_k[s * BLK : (s + 1) * BLK]
            sums[head][j, :, width:] = o[:, width:] + more_v[s * BLK : (s + 1) * BLK]
        dq = dq_t.astype(jnp.bfloat16).T
        out_ref[b, place(0, head), :width] = dq
        out_ref[b, place(0, head), width:] = out_t.astype(jnp.bfloat16).T
        return jnp.sum(dq.astype(jnp.float32) * q.astype(jnp.float32), axis=0, keepdims=True)

    for slots in ((2, 2), (3, 2), (3, 3), (4, 2), (4, 3), (4, 4)):

        @pl.when(jnp.logical_and(live[0] == slots[0], live[1] == slots[1]))
        def _():
            def keep(h, products):
                for s in range(slots[h]):
                    for n in range(2):
                        ahead[h][n, s] = products[n][s]

            def step(b, gain):
                done = []
                for h in range(heads):
                    products = [[ahead[h][n, s] for s in range(slots[h])] for n in range(2)]
                    after = h + 1 if h + 1 < heads else 0
                    at = b if h + 1 < heads else jnp.minimum(b + 1, blocks - 1)
                    keep(after, start(at, after, slots[after])[3])
                    low, ds = softmax(products)
                    q = in_ref[b, place(0, h), :width]
                    u = in_ref[b, place(0, h), width:]
                    chosen = [lists_ref[b, s, owned[h]] for s in range(slots[h])]
                    done.append(gain[h] + finish_block(b, h, q, (q, u), chosen, low, ds))
                return tuple(done)

            keep(0, start(0, 0, slots[0])[3])

            gain = lax.fori_loop(
                0, blocks, step, (jnp.zeros((1, width), jnp.float32),) * heads, unroll=4
            )
            for h in range(heads):
                gains_ref[h : h + 1] = gain[h]

    extra = parts(jnp.concatenate([gains_ref[h : h + 1] for h in range(heads)], axis=1))
    extra.append(jnp.zeros((SPARE - PARTS, both), jnp.bfloat16))
    extra = jnp.concatenate(extra, axis=0)

    def finish(j, carry):
        for head in range(heads):
            out_ref[j, place(1, head)] = sums[head][j].astype(jnp.bfloat16)
        out_ref[j, span:] = extra
        return carry

    lax.fori_loop(0, blocks, finish, 0, unroll=4)


def attention(mine, table, lists, live, arrived, heads):
    blocks, span, both = arrived.shape
    vmem = pl.BlockSpec(memory_space=pltpu.VMEM)
    smem = pl.BlockSpec(memory_space=pltpu.SMEM)
    return pl.pallas_call(
        attention_kernel,
        in_specs=[smem, smem, smem, pl.BlockSpec(memory_space=pl.ANY), vmem],
        out_specs=vmem,
        out_shape=jax.ShapeDtypeStruct((blocks, span + SPARE, both), jnp.bfloat16),
        scratch_shapes=[pltpu.VMEM((blocks, both, BLK), jnp.bfloat16)] * heads
        + [pltpu.VMEM((blocks, BLK, both), jnp.float32)] * heads
        + [pltpu.VMEM((2, lists.shape[1], BLK, BLK), jnp.float32)] * heads
        + [pltpu.VMEM((heads, both // 2), jnp.float32)]
        + [pltpu.SMEM(lists.shape, jnp.int32), pltpu.SemaphoreType.DMA(())],
        compiler_params=pltpu.CompilerParams(vmem_limit_bytes=24 << 20),
        name="attention",
    )(mine, table, live, lists, arrived)


def unpack_kernel(
    table_ref,
    back_hbm,
    q_hbm,
    k_hbm,
    qg_hbm,
    kg_hbm,
    out_hbm,
    dq_hbm,
    dk_hbm,
    dv_hbm,
    raw_ref,
    back_ref,
    gain_ref,
    done_ref,
    raw_sems,
    grad_sems,
    gain_sems,
    sems,
    copy_sems,
):
    groups, _, both = back_hbm.shape
    width = both // 2
    tokens, features = q_hbm.shape
    heads = features // (groups * width)
    step = tokens // CHUNKS
    loads = {}
    for n, raw_hbm in enumerate((q_hbm, k_hbm)):
        for c in range(CHUNKS):
            rows = pl.ds(c * step, step)
            some = [
                pltpu.make_async_copy(raw_hbm.at[rows], raw_ref.at[n, rows], raw_sems.at[n, c])
            ]
            for slot in range(heads):
                some.append(
                    pltpu.make_async_copy(
                        back_hbm.at[:, pl.ds((n * heads + slot) * tokens + c * step, step)],
                        back_ref.at[:, pl.ds((n * heads + slot) * tokens + c * step, step)],
                        grad_sems.at[n, c, slot],
                    )
                )
            if c == 0:
                gain_hbm = (qg_hbm, kg_hbm)[n]
                some.append(pltpu.make_async_copy(gain_hbm, gain_ref.at[n], gain_sems.at[n]))
            loads[n, c] = some
            for load in some:
                load.start()
    spots = [group_and_slot(table_ref[PLACE, h], groups) for h in range(groups * heads)]
    moves = []
    for n, (moved_hbm, hbm) in enumerate(((out_hbm, dq_hbm), (dv_hbm, dk_hbm))):
        places = []
        for c in range(CHUNKS):
            for load in loads[n, c]:
                load.wait()
        for head, (group, slot) in enumerate(spots):
            first = pl.multiple_of((n * heads + slot) * tokens, tokens)
            places.append((group, first))
            move = pltpu.make_async_copy(
                back_ref.at[group, pl.ds(first, tokens), pl.ds(width, width)],
                moved_hbm.at[:, pl.ds(head * width, width)],
                copy_sems.at[head, n],
            )
            move.start()
            moves.append(move)
        for c in range(CHUNKS):

            def some_rows(i, carry):
                row = pl.multiple_of(c * step + i * ROWS, ROWS)
                x = raw_ref[n, pl.ds(row, ROWS)].astype(jnp.float32)
                inverse = inverse_rms(x)
                unit = x * inverse
                pieces = []
                for group, first in places:
                    at = pl.multiple_of(first + row, ROWS)
                    pieces.append(back_ref[group, pl.ds(at, ROWS), :width])
                g = jnp.concatenate(pieces, axis=-1).astype(jnp.float32) * gain_ref[n]
                mean = jnp.mean(g * unit, axis=-1, keepdims=True)
                done_ref[n, pl.ds(row, ROWS)] = (inverse * (g - unit * mean)).astype(jnp.bfloat16)
                return carry

            lax.fori_loop(0, step // ROWS, some_rows, 0)
            move = pltpu.make_async_copy(
                done_ref.at[n, pl.ds(c * step, step)], hbm.at[pl.ds(c * step, step)], sems.at[n, c]
            )
            move.start()
            moves.append(move)
    for move in moves:
        move.wait()


def unpack(table, back, q, k, q_gain, k_gain):
    groups, _, both = back.shape
    tokens, features = q.shape
    heads = 2 * features // (groups * both)
    hbm = pl.BlockSpec(memory_space=pltpu.HBM)
    return pl.pallas_call(
        unpack_kernel,
        in_specs=[pl.BlockSpec(memory_space=pltpu.SMEM)] + [hbm] * 5,
        out_specs=[hbm] * 4,
        out_shape=[jax.ShapeDtypeStruct((tokens, features), jnp.bfloat16)] * 4,
        scratch_shapes=[
            pltpu.VMEM((2, tokens, features), jnp.bfloat16),
            pltpu.VMEM((groups, 2 * heads * tokens, both), jnp.bfloat16),
            pltpu.VMEM((2, 1, features), jnp.float32),
            pltpu.VMEM((2, tokens, features), jnp.bfloat16),
            pltpu.SemaphoreType.DMA((2, CHUNKS)),
            pltpu.SemaphoreType.DMA((2, CHUNKS, heads)),
            pltpu.SemaphoreType.DMA((2,)),
            pltpu.SemaphoreType.DMA((2, CHUNKS)),
            pltpu.SemaphoreType.DMA((groups * heads, 2)),
        ],
        compiler_params=pltpu.CompilerParams(vmem_limit_bytes=16 << 20),
        name="unpack",
    )(table, *(in_hbm(x) for x in (back, q, k, q_gain[None], k_gain[None])))


def gains_kernel(table_ref, back_hbm, out_ref, extra_ref, sem):
    groups, rows, _ = back_hbm.shape
    copies, heads, width = out_ref.shape
    load = pltpu.make_async_copy(back_hbm.at[:, pl.ds(rows - SPARE, SPARE)], extra_ref, sem)
    load.start()
    load.wait()
    for head in range(heads):
        group, slot = group_and_slot(table_ref[PLACE, head], groups)
        extra = extra_ref[group].astype(jnp.float32)
        total = extra[0:1]
        for n in range(1, PARTS):
            total = total + extra[n : n + 1]
        out_ref[0, head : head + 1] = jnp.where(slot == 0, total[:, :width], total[:, width:])
    for copy in range(1, copies):
        out_ref[copy] = out_ref[0]


def gain_sums(table, back, copies):
    groups, _, both = back.shape
    return pl.pallas_call(
        gains_kernel,
        in_specs=[pl.BlockSpec(memory_space=pltpu.SMEM), pl.BlockSpec(memory_space=pltpu.HBM)],
        out_specs=pl.BlockSpec(memory_space=pltpu.VMEM),
        out_shape=jax.ShapeDtypeStruct((copies, table.shape[1], BLK), jnp.float32),
        scratch_shapes=[
            pltpu.VMEM((groups, SPARE, both), jnp.bfloat16),
            pltpu.SemaphoreType.DMA(()),
        ],
        compiler_params=pltpu.CompilerParams(vmem_limit_bytes=2 << 20),
        name="gains",
    )(table, in_hbm(back))


def last_kernel(terms_ref, qg_ref, kg_ref, q_ref, k_ref):
    total = terms_ref[0]
    for n in range(1, terms_ref.shape[0]):
        total = total + terms_ref[n]
    q_ref[...] = total / qg_ref[...]
    k_ref[...] = total / kg_ref[...]


def last(terms, q_gain, k_gain):
    shape = terms.shape[1:]
    vmem = pl.BlockSpec(memory_space=pltpu.VMEM)
    q, k = pl.pallas_call(
        last_kernel,
        in_specs=[vmem] * 3,
        out_specs=[vmem] * 2,
        out_shape=[jax.ShapeDtypeStruct(shape, jnp.float32)] * 2,
        compiler_params=pltpu.CompilerParams(vmem_limit_bytes=2 << 20),
        name="last",
    )(terms, q_gain.reshape(shape), k_gain.reshape(shape))
    return q.reshape(-1), k.reshape(-1)


def shards(query_raw, key_raw, value, upstream, query_gain, key_gain, key_blocks, live):
    groups = lax.axis_size("seq")
    heads = key_blocks.shape[1] // groups
    mine = lax.axis_index("seq").reshape(1)
    lists = jnp.transpose(key_blocks[0], (1, 2, 0))
    packed, table = pack(
        live, query_raw[0], key_raw[0], value[0], upstream[0], query_gain, key_gain, groups, heads
    )
    packed, mine = lax.optimization_barrier((packed, mine))
    arrived = lax.all_to_all(packed, "seq", split_axis=0, concat_axis=0, tiled=True)
    results = attention(mine, table, lists, live, arrived, heads)
    back = lax.all_to_all(results, "seq", split_axis=0, concat_axis=0, tiled=True)
    copies = gain_sums(table, back, lax.axis_size("clip"))
    terms = lax.all_to_all(copies, "clip", split_axis=0, concat_axis=0, tiled=True)
    attended, grad_query, grad_key, grad_value = unpack(
        table, back, query_raw[0], key_raw[0], query_gain, key_gain
    )
    q_total, k_total = last(terms, query_gain, key_gain)
    return (
        attended[None],
        grad_query[None],
        grad_key[None],
        grad_value[None],
        q_total,
        k_total,
    )


def solution(mesh):
    tokens = P("clip", "seq", None)
    return jax.shard_map(
        shards,
        mesh=mesh,
        in_specs=(tokens,) * 4 + (P(), P(), P("clip", None, None, None), P("clip", None)),
        out_specs=(tokens,) * 4 + (P(), P()),
        check_vma=False,
    )
```

```python
import jax
import jax.numpy as jnp
from jax import lax
from jax.experimental import pallas as pl
from jax.experimental.pallas import tpu as pltpu
from jax.sharding import PartitionSpec as P

BLK = 128
EPSILON = 1e-06
ROWS = 64
CHUNKS = 2
PARTS = 3
SPARE = 8
PLACE, ORDER = range(2)
QUERY, COTANGENT, KEY, VALUE = range(4)
GRAD_Q, OUT, GRAD_K, GRAD_V = range(4)
LOG2E = 1.4426950408889634


def contract(a, b, dims):
    return lax.dot_general(a, b, (dims, ((), ())), preferred_element_type=jnp.float32)


def inverse_rms(x):
    return lax.rsqrt(jnp.mean(x * x, axis=-1, keepdims=True) + EPSILON)


def rank_heads(live_ref, table_ref):
    count = table_ref.shape[1]
    lives = [live_ref[0, h] for h in range(count)]
    fours = [(n >= 4).astype(jnp.int32) for n in lives]
    somes = [(n >= 3).astype(jnp.int32) for n in lives]
    four, three, two = jnp.int32(0), sum(fours), sum(somes)
    for h in range(count):
        rank = jnp.where(fours[h] == 1, four, jnp.where(somes[h] == 1, three, two))
        table_ref[PLACE, h] = rank
        table_ref[ORDER, rank] = h
        four = four + fours[h]
        three = three + somes[h] - fours[h]
        two = two + 1 - somes[h]


def group_and_slot(rank, groups):
    second = rank >= groups
    return jnp.where(second, 2 * groups - 1 - rank, rank), second.astype(jnp.int32)


def pack_kernel(
    live_hbm,
    q_hbm,
    k_hbm,
    v_hbm,
    u_hbm,
    qg_hbm,
    kg_hbm,
    out_ref,
    table_ref,
    raw_ref,
    gain_ref,
    live_ref,
    raw_sems,
    gain_sems,
    copy_sems,
    live_sem,
):
    groups, span, both = out_ref.shape
    width = both // 2
    tokens = raw_ref.shape[1]
    heads = span // (2 * tokens)
    step = tokens // CHUNKS

    loads = [
        [
            pltpu.make_async_copy(
                hbm.at[pl.ds(c * step, step)],
                raw_ref.at[n, pl.ds(c * step, step)],
                raw_sems.at[n, c],
            )
            for c in range(CHUNKS)
        ]
        for n, hbm in enumerate((q_hbm, k_hbm))
    ]
    gain_loads = [
        pltpu.make_async_copy(hbm, gain_ref.at[n], gain_sems.at[n])
        for n, hbm in enumerate((qg_hbm, kg_hbm))
    ]
    live_load = pltpu.make_async_copy(live_hbm, live_ref, live_sem)
    live_load.start()
    for n in range(2):
        gain_loads[n].start()
        loads[n][0].start()
    for c in range(1, CHUNKS):
        for n in range(2):
            loads[n][c].start()
    live_load.wait()
    rank_heads(live_ref, table_ref)
    moves, spots = [], []
    for head in range(groups * heads):
        group, slot = group_and_slot(table_ref[PLACE, head], groups)
        spots.append((group, slot))
        for n, (hbm, pair) in enumerate(((u_hbm, 0), (v_hbm, 1))):
            first = pl.multiple_of((pair * heads + slot) * tokens, tokens)
            moves.append(
                pltpu.make_async_copy(
                    hbm.at[:, pl.ds(head * width, width)],
                    out_ref.at[group, pl.ds(first, tokens), pl.ds(width, width)],
                    copy_sems.at[head, n],
                )
            )
    for move in moves:
        move.start()
    for c in range(CHUNKS):
        for n in range(2):
            if c == 0:
                gain_loads[n].wait()
            loads[n][c].wait()

            def some_rows(i, carry):
                row = pl.multiple_of(c * step + i * ROWS, ROWS)
                x = raw_ref[n, pl.ds(row, ROWS)].astype(jnp.float32)
                y = (x * inverse_rms(x) * gain_ref[n]).astype(jnp.bfloat16)
                for head, (group, slot) in enumerate(spots):
                    first = pl.multiple_of((n * heads + slot) * tokens + row, ROWS)
                    at = head * width
                    out_ref[group, pl.ds(first, ROWS), :width] = y[:, at : at + width]
                return carry

            lax.fori_loop(0, step // ROWS, some_rows, 0)
    for move in moves:
        move.wait()


def in_hbm(x):
    return pltpu.with_memory_space_constraint(x, pltpu.HBM)


def pack(live, q, k, v, u, q_gain, k_gain, groups, heads):
    tokens, features = q.shape
    width = features // (groups * heads)
    hbm = pl.BlockSpec(memory_space=pltpu.HBM)
    vmem = pl.BlockSpec(memory_space=pltpu.VMEM)
    return pl.pallas_call(
        pack_kernel,
        in_specs=[hbm] * 7,
        out_specs=[vmem, pl.BlockSpec(memory_space=pltpu.SMEM)],
        out_shape=[
            jax.ShapeDtypeStruct((groups, 2 * heads * tokens, 2 * width), jnp.bfloat16),
            jax.ShapeDtypeStruct((2, groups * heads), jnp.int32),
        ],
        scratch_shapes=[
            pltpu.VMEM((2, tokens, features), jnp.bfloat16),
            pltpu.VMEM((2, 1, features), jnp.float32),
            pltpu.SMEM(live.shape, jnp.int32),
            pltpu.SemaphoreType.DMA((2, CHUNKS)),
            pltpu.SemaphoreType.DMA((2,)),
            pltpu.SemaphoreType.DMA((groups * heads, 2)),
            pltpu.SemaphoreType.DMA(()),
        ],
        compiler_params=pltpu.CompilerParams(vmem_limit_bytes=12 << 20),
        name="pack",
    )(*(in_hbm(x) for x in (live, q, k, v, u, q_gain[None], k_gain[None])))


def attention_kernel(mine_ref, table_ref, live_ref, lists_any, in_ref, out_ref, *scratch):
    *scratch, lists_ref, lists_sem = scratch
    lists_load = pltpu.make_async_copy(lists_any, lists_ref, lists_sem)
    lists_load.start()
    blocks, span, both = in_ref.shape
    heads = len(scratch) // 3
    width = both // 2
    scale = width ** (-0.5)
    turned, sums, ahead, gains_ref = scratch[:heads], scratch[heads : 2 * heads], scratch[2 * heads : -1], scratch[-1]
    mine = mine_ref[0]
    owned = [table_ref[ORDER, rank] for rank in (mine, 2 * blocks - 1 - mine)]
    live = [live_ref[0, h] for h in owned]

    def place(pair, head):
        return pl.ds((pair * heads + head) * BLK, BLK)

    def parts(row):
        pieces = []
        for _ in range(PARTS):
            pieces.append(row.astype(jnp.bfloat16))
            row = row - pieces[-1].astype(jnp.float32)
        return pieces

    def prepare(j, carry):
        for head in range(heads):
            turned[head][j] = in_ref[j, place(1, head)].T
            sums[head][j] = jnp.zeros((BLK, both), jnp.float32)
        return carry

    lax.fori_loop(0, blocks, prepare, 0, unroll=4)
    lists_load.wait()

    def start(b, head, slots):
        q = in_ref[b, place(0, head), :width]
        u = in_ref[b, place(0, head), width:]
        diagonal = (q, u)
        chosen = [lists_ref[b, s, owned[head]] for s in range(slots)]
        rows = jnp.concatenate([in_ref[j, place(1, head)] for j in chosen], axis=0)
        scores = contract(rows[:, :width], q, ((1,), (1,)))
        grads = contract(rows[:, width:], u, ((1,), (1,)))
        products = ([scores[s * BLK : (s + 1) * BLK] for s in range(slots)], [grads[s * BLK : (s + 1) * BLK] for s in range(slots)])
        return q, diagonal, chosen, products

    def softmax(products):
        scores, grads = products
        factor = scale * LOG2E
        tops = [jnp.max(s, axis=0, keepdims=True) * factor for s in scores]
        top = tops[0]
        for t in tops[1:]:
            top = jnp.maximum(top, t)
        raised = [jnp.exp2(s * factor - top) for s in scores]
        total = raised[0]
        inner = raised[0] * grads[0]
        for e, g in zip(raised[1:], grads[1:]):
            total = total + e
            inner = inner + e * g
        inverse = 1.0 / jnp.sum(total, axis=0, keepdims=True)
        delta = jnp.sum(inner, axis=0, keepdims=True) * inverse
        probs = [e * inverse for e in raised]
        low = [p.astype(jnp.bfloat16) for p in probs]
        ds = [(p * ((g - delta) * scale)).astype(jnp.bfloat16) for p, g in zip(probs, grads)]
        return low, ds

    def finish_block(b, head, q, diagonal, chosen, low, ds):
        keys = jnp.concatenate([turned[head][j, :width] for j in chosen], axis=1)
        values = jnp.concatenate([turned[head][j, width:] for j in chosen], axis=1)
        out_t = contract(values, jnp.concatenate(low, axis=0), ((1,), (0,)))
        dq_t = contract(keys, jnp.concatenate(ds, axis=0), ((1,), (0,)))
        q, u = diagonal
        more_k = contract(jnp.concatenate(ds, axis=0), q, ((1,), (0,)))
        more_v = contract(jnp.concatenate(low, axis=0), u, ((1,), (0,)))
        old = [sums[head][j] for j in chosen]
        for s, (j, o) in enumerate(zip(chosen, old)):
            sums[head][j, :, :width] = o[:, :width] + more_k[s * BLK : (s + 1) * BLK]
            sums[head][j, :, width:] = o[:, width:] + more_v[s * BLK : (s + 1) * BLK]
        dq = dq_t.astype(jnp.bfloat16).T
        out_ref[b, place(0, head), :width] = dq
        out_ref[b, place(0, head), width:] = out_t.astype(jnp.bfloat16).T
        return jnp.sum(dq.astype(jnp.float32) * q.astype(jnp.float32), axis=0, keepdims=True)

    for slots in ((2, 2), (3, 2), (3, 3), (4, 2), (4, 3), (4, 4)):

        @pl.when(jnp.logical_and(live[0] == slots[0], live[1] == slots[1]))
        def _():
            def keep(h, products):
                for s in range(slots[h]):
                    for n in range(2):
                        ahead[h][n, s] = products[n][s]

            def step(b, gain):
                done = []
                for h in range(heads):
                    products = [[ahead[h][n, s] for s in range(slots[h])] for n in range(2)]
                    after = h + 1 if h + 1 < heads else 0
                    at = b if h + 1 < heads else jnp.minimum(b + 1, blocks - 1)
                    keep(after, start(at, after, slots[after])[3])
                    low, ds = softmax(products)
                    q = in_ref[b, place(0, h), :width]
                    u = in_ref[b, place(0, h), width:]
                    chosen = [lists_ref[b, s, owned[h]] for s in range(slots[h])]
                    done.append(gain[h] + finish_block(b, h, q, (q, u), chosen, low, ds))
                return tuple(done)

            keep(0, start(0, 0, slots[0])[3])

            gain = lax.fori_loop(
                0, blocks, step, (jnp.zeros((1, width), jnp.float32),) * heads, unroll=4
            )
            for h in range(heads):
                gains_ref[h : h + 1] = gain[h]

    extra = parts(jnp.concatenate([gains_ref[h : h + 1] for h in range(heads)], axis=1))
    names = [jnp.zeros((1, width), jnp.float32) + h.astype(jnp.float32) for h in owned]
    extra.append(jnp.concatenate(names, axis=1).astype(jnp.bfloat16))
    extra.append(jnp.zeros((SPARE - PARTS - 1, both), jnp.bfloat16))
    extra = jnp.concatenate(extra, axis=0)

    def finish(j, carry):
        for head in range(heads):
            out_ref[j, place(1, head)] = sums[head][j].astype(jnp.bfloat16)
        out_ref[j, span:] = extra
        return carry

    lax.fori_loop(0, blocks, finish, 0, unroll=4)


def attention(mine, table, lists, live, arrived, heads):
    blocks, span, both = arrived.shape
    vmem = pl.BlockSpec(memory_space=pltpu.VMEM)
    smem = pl.BlockSpec(memory_space=pltpu.SMEM)
    return pl.pallas_call(
        attention_kernel,
        in_specs=[smem, smem, smem, pl.BlockSpec(memory_space=pl.ANY), vmem],
        out_specs=vmem,
        out_shape=jax.ShapeDtypeStruct((blocks, span + SPARE, both), jnp.bfloat16),
        scratch_shapes=[pltpu.VMEM((blocks, both, BLK), jnp.bfloat16)] * heads
        + [pltpu.VMEM((blocks, BLK, both), jnp.float32)] * heads
        + [pltpu.VMEM((2, lists.shape[1], BLK, BLK), jnp.float32)] * heads
        + [pltpu.VMEM((heads, both // 2), jnp.float32)]
        + [pltpu.SMEM(lists.shape, jnp.int32), pltpu.SemaphoreType.DMA(())],
        compiler_params=pltpu.CompilerParams(vmem_limit_bytes=24 << 20),
        name="attention",
    )(mine, table, live, lists, arrived)


def unpack_kernel(
    table_ref,
    back_ref,
    q_ref,
    k_ref,
    qg_ref,
    kg_ref,
    out_hbm,
    dq_hbm,
    dk_hbm,
    dv_hbm,
    done_ref,
    sems,
    copy_sems,
):
    groups, _, both = back_ref.shape
    width = both // 2
    tokens, features = q_ref.shape
    heads = features // (groups * width)
    step = tokens // CHUNKS
    moves, spots = [], []
    for head in range(groups * heads):
        group, slot = group_and_slot(table_ref[PLACE, head], groups)
        spots.append((group, slot))
        for n, hbm in enumerate((out_hbm, dv_hbm)):
            first = pl.multiple_of((n * heads + slot) * tokens, tokens)
            moves.append(
                pltpu.make_async_copy(
                    back_ref.at[group, pl.ds(first, tokens), pl.ds(width, width)],
                    hbm.at[:, pl.ds(head * width, width)],
                    copy_sems.at[head, n],
                )
            )
    for move in moves:
        move.start()
    for c in range(CHUNKS):
        for n, (raw_ref, gain_ref, hbm) in enumerate(
            ((q_ref, qg_ref, dq_hbm), (k_ref, kg_ref, dk_hbm))
        ):

            def some_rows(i, carry):
                row = pl.multiple_of(c * step + i * ROWS, ROWS)
                x = raw_ref[pl.ds(row, ROWS)].astype(jnp.float32)
                inverse = inverse_rms(x)
                unit = x * inverse
                pieces = []
                for group, slot in spots:
                    first = pl.multiple_of((n * heads + slot) * tokens + row, ROWS)
                    pieces.append(back_ref[group, pl.ds(first, ROWS), :width])
                grads = jnp.concatenate(pieces, axis=-1)
                g = grads.astype(jnp.float32) * gain_ref[...]
                mean = jnp.mean(g * unit, axis=-1, keepdims=True)
                done_ref[n, pl.ds(row, ROWS)] = (inverse * (g - unit * mean)).astype(jnp.bfloat16)
                return carry

            lax.fori_loop(0, step // ROWS, some_rows, 0)
            move = pltpu.make_async_copy(
                done_ref.at[n, pl.ds(c * step, step)], hbm.at[pl.ds(c * step, step)], sems.at[n, c]
            )
            move.start()
            moves.append(move)
    for move in moves:
        move.wait()


def unpack(table, back, q, k, q_gain, k_gain):
    groups, _, both = back.shape
    tokens, features = q.shape
    hbm = pl.BlockSpec(memory_space=pltpu.HBM)
    vmem = pl.BlockSpec(memory_space=pltpu.VMEM)
    return pl.pallas_call(
        unpack_kernel,
        in_specs=[pl.BlockSpec(memory_space=pltpu.SMEM)] + [vmem] * 5,
        out_specs=[hbm] * 4,
        out_shape=[jax.ShapeDtypeStruct((tokens, features), jnp.bfloat16)] * 4,
        scratch_shapes=[
            pltpu.VMEM((2, tokens, features), jnp.bfloat16),
            pltpu.SemaphoreType.DMA((2, CHUNKS)),
            pltpu.SemaphoreType.DMA((2 * features // both, 2)),
        ],
        compiler_params=pltpu.CompilerParams(vmem_limit_bytes=12 << 20),
        name="unpack",
    )(table, back, q, k, q_gain[None], k_gain[None])


def gains_kernel(back_ref, out_ref):
    groups, rows, both = back_ref.shape
    heads, width = out_ref.shape
    order = lax.broadcasted_iota(jnp.int32, (heads, width), 0).astype(jnp.float32)
    whole = jnp.zeros((heads, width), jnp.float32)
    for group in range(groups):
        extra = back_ref[group, rows - SPARE :].astype(jnp.float32)
        total = extra[0:1]
        for n in range(1, PARTS):
            total = total + extra[n : n + 1]
        names = extra[PARTS : PARTS + 1]
        for at in range(0, both, width):
            mine = order == names[:, at : at + width]
            whole = jnp.where(mine, total[:, at : at + width], whole)
    out_ref[...] = whole


def add_kernel(a_ref, b_ref, out_ref):
    out_ref[...] = a_ref[...] + b_ref[...]


def last_kernel(a_ref, b_ref, c_ref, d_ref, qg_ref, kg_ref, q_ref, k_ref):
    total = (a_ref[...] + b_ref[...]) + (c_ref[...] + d_ref[...])
    q_ref[...] = total / qg_ref[...]
    k_ref[...] = total / kg_ref[...]


def small_call(kernel, shapes, name, *args):
    return pl.pallas_call(
        kernel,
        in_specs=[pl.BlockSpec(memory_space=pltpu.VMEM)] * len(args),
        out_specs=[pl.BlockSpec(memory_space=pltpu.VMEM)] * len(shapes),
        out_shape=[jax.ShapeDtypeStruct(shape, jnp.float32) for shape in shapes],
        compiler_params=pltpu.CompilerParams(vmem_limit_bytes=2 << 20),
        name=name,
    )(*args)


def clip_gains(back, q_gain, k_gain):
    size = lax.axis_size("clip")
    rows = q_gain.shape[0] // BLK
    (one,) = small_call(gains_kernel, [(rows, BLK)], "gains", back)
    other = lax.ppermute(one, "clip", [(i, i ^ 1) for i in range(size)])
    (two,) = small_call(add_kernel, [(rows, BLK)], "add", one, other)
    terms = [
        lax.ppermute(two, "clip", [(i, (i + hop) % size) for i in range(size)]) for hop in (4, 2, 6)
    ]
    q, k = small_call(
        last_kernel,
        [(rows, BLK)] * 2,
        "last",
        two,
        *terms,
        q_gain.reshape(rows, BLK),
        k_gain.reshape(rows, BLK),
    )
    return q.reshape(-1), k.reshape(-1)


def shards(query_raw, key_raw, value, upstream, query_gain, key_gain, key_blocks, live):
    groups = lax.axis_size("seq")
    heads = key_blocks.shape[1] // groups
    mine = lax.axis_index("seq").reshape(1)
    lists = jnp.transpose(key_blocks[0], (1, 2, 0))
    packed, table = pack(
        live, query_raw[0], key_raw[0], value[0], upstream[0], query_gain, key_gain, groups, heads
    )
    packed, mine = lax.optimization_barrier((packed, mine))
    arrived = lax.all_to_all(packed, "seq", split_axis=0, concat_axis=0, tiled=True)
    results = attention(mine, table, lists, live, arrived, heads)
    back = lax.all_to_all(results, "seq", split_axis=0, concat_axis=0, tiled=True)
    attended, grad_query, grad_key, grad_value = unpack(
        table, back, query_raw[0], key_raw[0], query_gain, key_gain
    )
    q_total, k_total = clip_gains(back, query_gain, key_gain)
    return (
        attended[None],
        grad_query[None],
        grad_key[None],
        grad_value[None],
        q_total,
        k_total,
    )


def solution(mesh):
    tokens = P("clip", "seq", None)
    return jax.shard_map(
        shards,
        mesh=mesh,
        in_specs=(tokens,) * 4 + (P(), P(), P("clip", None, None, None), P("clip", None)),
        out_specs=(tokens,) * 4 + (P(), P()),
        check_vma=False,
    )
```

```python
import jax
import jax.numpy as jnp
from jax import lax
from jax.experimental import pallas as pl
from jax.experimental.pallas import tpu as pltpu
from jax.sharding import PartitionSpec as P

BLK = 128
EPSILON = 1e-06
ROWS = 64
CHUNKS = 2
PARTS = 3
SPARE = 8
UNROLL = 4
PLACE, ORDER = range(2)
QUERY, COTANGENT, KEY, VALUE = range(4)
GRAD_Q, OUT, GRAD_K, GRAD_V = range(4)
LOG2E = 1.4426950408889634


def contract(a, b, dims):
    return lax.dot_general(a, b, (dims, ((), ())), preferred_element_type=jnp.float32)


def inverse_rms(x):
    return lax.rsqrt(jnp.mean(x * x, axis=-1, keepdims=True) + EPSILON)


def rank_heads(live_ref, table_ref):
    count = table_ref.shape[1]
    lives = [live_ref[0, h] for h in range(count)]
    fours = [(n >= 4).astype(jnp.int32) for n in lives]
    somes = [(n >= 3).astype(jnp.int32) for n in lives]
    four, three, two = jnp.int32(0), sum(fours), sum(somes)
    for h in range(count):
        rank = jnp.where(fours[h] == 1, four, jnp.where(somes[h] == 1, three, two))
        table_ref[PLACE, h] = rank
        table_ref[ORDER, rank] = h
        four = four + fours[h]
        three = three + somes[h] - fours[h]
        two = two + 1 - somes[h]


def group_and_slot(rank, groups):
    second = rank >= groups
    return jnp.where(second, 2 * groups - 1 - rank, rank), second.astype(jnp.int32)


def pack_kernel(
    live_hbm,
    q_hbm,
    k_hbm,
    v_hbm,
    u_hbm,
    qg_hbm,
    kg_hbm,
    out_ref,
    table_ref,
    raw_ref,
    gain_ref,
    live_ref,
    raw_sems,
    gain_sems,
    copy_sems,
    live_sem,
):
    groups, span, both = out_ref.shape
    width = both // 2
    tokens = raw_ref.shape[1]
    heads = span // (2 * tokens)
    step = tokens // CHUNKS

    loads = [
        [
            pltpu.make_async_copy(
                hbm.at[pl.ds(c * step, step)],
                raw_ref.at[n, pl.ds(c * step, step)],
                raw_sems.at[n, c],
            )
            for c in range(CHUNKS)
        ]
        for n, hbm in enumerate((q_hbm, k_hbm))
    ]
    gain_loads = [
        pltpu.make_async_copy(hbm, gain_ref.at[n], gain_sems.at[n])
        for n, hbm in enumerate((qg_hbm, kg_hbm))
    ]
    live_load = pltpu.make_async_copy(live_hbm, live_ref, live_sem)
    live_load.start()
    for n in range(2):
        gain_loads[n].start()
        loads[n][0].start()
    for c in range(1, CHUNKS):
        for n in range(2):
            loads[n][c].start()
    live_load.wait()
    rank_heads(live_ref, table_ref)
    moves, spots = [], []
    for head in range(groups * heads):
        group, slot = group_and_slot(table_ref[PLACE, head], groups)
        spots.append((group, slot))
        for n, (hbm, pair) in enumerate(((u_hbm, 0), (v_hbm, 1))):
            first = pl.multiple_of((pair * heads + slot) * tokens, tokens)
            moves.append(
                pltpu.make_async_copy(
                    hbm.at[:, pl.ds(head * width, width)],
                    out_ref.at[group, pl.ds(first, tokens), pl.ds(width, width)],
                    copy_sems.at[head, n],
                )
            )
    for move in moves:
        move.start()
    for c in range(CHUNKS):
        for n in range(2):
            if c == 0:
                gain_loads[n].wait()
            loads[n][c].wait()

            def some_rows(i, carry):
                row = pl.multiple_of(c * step + i * ROWS, ROWS)
                x = raw_ref[n, pl.ds(row, ROWS)].astype(jnp.float32)
                y = (x * inverse_rms(x) * gain_ref[n]).astype(jnp.bfloat16)
                for head, (group, slot) in enumerate(spots):
                    first = pl.multiple_of((n * heads + slot) * tokens + row, ROWS)
                    at = head * width
                    out_ref[group, pl.ds(first, ROWS), :width] = y[:, at : at + width]
                return carry

            lax.fori_loop(0, step // ROWS, some_rows, 0)
    for move in moves:
        move.wait()


def in_hbm(x):
    return pltpu.with_memory_space_constraint(x, pltpu.HBM)


def pack(live, q, k, v, u, q_gain, k_gain, groups, heads):
    tokens, features = q.shape
    width = features // (groups * heads)
    hbm = pl.BlockSpec(memory_space=pltpu.HBM)
    vmem = pl.BlockSpec(memory_space=pltpu.VMEM)
    return pl.pallas_call(
        pack_kernel,
        in_specs=[hbm] * 7,
        out_specs=[vmem, pl.BlockSpec(memory_space=pltpu.SMEM)],
        out_shape=[
            jax.ShapeDtypeStruct((groups, 2 * heads * tokens, 2 * width), jnp.bfloat16),
            jax.ShapeDtypeStruct((2, groups * heads), jnp.int32),
        ],
        scratch_shapes=[
            pltpu.VMEM((2, tokens, features), jnp.bfloat16),
            pltpu.VMEM((2, 1, features), jnp.float32),
            pltpu.SMEM(live.shape, jnp.int32),
            pltpu.SemaphoreType.DMA((2, CHUNKS)),
            pltpu.SemaphoreType.DMA((2,)),
            pltpu.SemaphoreType.DMA((groups * heads, 2)),
            pltpu.SemaphoreType.DMA(()),
        ],
        compiler_params=pltpu.CompilerParams(vmem_limit_bytes=12 << 20),
        name="pack",
    )(*(in_hbm(x) for x in (live, q, k, v, u, q_gain[None], k_gain[None])))


def attention_kernel(mine_ref, table_ref, live_ref, lists_any, in_ref, out_ref, *scratch):
    *scratch, waiting, lists_ref, lists_sem = scratch
    lists_load = pltpu.make_async_copy(lists_any, lists_ref, lists_sem)
    lists_load.start()
    blocks, span, both = in_ref.shape
    heads = len(scratch) // 3
    width = both // 2
    scale = width ** (-0.5)
    turned, sums, ahead, gains_ref = scratch[:heads], scratch[heads : 2 * heads], scratch[2 * heads : -1], scratch[-1]
    mine = mine_ref[0]
    owned = [table_ref[ORDER, rank] for rank in (mine, 2 * blocks - 1 - mine)]
    live = [live_ref[0, h] for h in owned]

    def place(pair, head):
        return pl.ds((pair * heads + head) * BLK, BLK)

    def parts(row):
        pieces = []
        for _ in range(PARTS):
            pieces.append(row.astype(jnp.bfloat16))
            row = row - pieces[-1].astype(jnp.float32)
        return pieces

    def prepare(j, carry):
        for head in range(heads):
            turned[head][j] = in_ref[j, place(1, head)].T
            sums[head][j] = jnp.zeros((BLK, both), jnp.float32)
        return carry

    lax.fori_loop(0, blocks, prepare, 0, unroll=4)
    lists_load.wait()

    def start(b, head, slots):
        q = in_ref[b, place(0, head), :width]
        u = in_ref[b, place(0, head), width:]
        diagonal = (q, u)
        chosen = [lists_ref[b, s, owned[head]] for s in range(slots)]
        rows = jnp.concatenate([in_ref[j, place(1, head)] for j in chosen], axis=0)
        scores = contract(rows[:, :width], q, ((1,), (1,)))
        grads = contract(rows[:, width:], u, ((1,), (1,)))
        products = ([scores[s * BLK : (s + 1) * BLK] for s in range(slots)], [grads[s * BLK : (s + 1) * BLK] for s in range(slots)])
        return q, diagonal, chosen, products

    def softmax(products):
        scores, grads = products
        factor = scale * LOG2E
        tops = [jnp.max(s, axis=0, keepdims=True) * factor for s in scores]
        top = tops[0]
        for t in tops[1:]:
            top = jnp.maximum(top, t)
        raised = [jnp.exp2(s * factor - top) for s in scores]
        total = raised[0]
        inner = raised[0] * grads[0]
        for e, g in zip(raised[1:], grads[1:]):
            total = total + e
            inner = inner + e * g
        inverse = 1.0 / jnp.sum(total, axis=0, keepdims=True)
        delta = jnp.sum(inner, axis=0, keepdims=True) * inverse
        probs = [e * inverse for e in raised]
        low = [p.astype(jnp.bfloat16) for p in probs]
        ds = [(p * ((g - delta) * scale)).astype(jnp.bfloat16) for p, g in zip(probs, grads)]
        return low, ds

    def finish_block(b, head, q, diagonal, chosen, low, ds):
        keys = jnp.concatenate([turned[head][j, :width] for j in chosen], axis=1)
        values = jnp.concatenate([turned[head][j, width:] for j in chosen], axis=1)
        out_t = contract(values, jnp.concatenate(low, axis=0), ((1,), (0,)))
        dq_t = contract(keys, jnp.concatenate(ds, axis=0), ((1,), (0,)))
        q, u = diagonal
        more_k = contract(jnp.concatenate(ds, axis=0), q, ((1,), (0,)))
        more_v = contract(jnp.concatenate(low, axis=0), u, ((1,), (0,)))
        old = [sums[head][j] for j in chosen]
        for s, (j, o) in enumerate(zip(chosen, old)):
            sums[head][j, :, :width] = o[:, :width] + more_k[s * BLK : (s + 1) * BLK]
            sums[head][j, :, width:] = o[:, width:] + more_v[s * BLK : (s + 1) * BLK]
        dq = dq_t.astype(jnp.bfloat16).T
        out_ref[b, place(0, head), :width] = dq
        out_ref[b, place(0, head), width:] = out_t.astype(jnp.bfloat16).T
        return jnp.sum(dq.astype(jnp.float32) * q.astype(jnp.float32), axis=0, keepdims=True)

    for slots in ((2, 2), (3, 2), (3, 3), (4, 2), (4, 3), (4, 4)):

        @pl.when(jnp.logical_and(live[0] == slots[0], live[1] == slots[1]))
        def _():
            def keep(h, products):
                for s in range(slots[h]):
                    for n in range(2):
                        ahead[h][n, s] = products[n][s]

            last_head = heads - 1

            def complete(b, h, low, ds):
                rows = in_ref[b, place(0, h)]
                q, u = rows[:, :width], rows[:, width:]
                chosen = [lists_ref[b, s, owned[h]] for s in range(slots[h])]
                return finish_block(b, h, q, (q, u), chosen, low, ds)

            def step(i, gain):
                gain = list(gain)
                before = jnp.maximum(UNROLL * i - 1, 0)
                pending = (
                    before,
                    last_head,
                    [waiting[0, s] for s in range(slots[last_head])],
                    [waiting[1, s] for s in range(slots[last_head])],
                )
                for k in range(UNROLL):
                    b = UNROLL * i + k
                    for h in range(heads):
                        products = [[ahead[h][n, s] for s in range(slots[h])] for n in range(2)]
                        after = h + 1 if h + 1 < heads else 0
                        at = b if h + 1 < heads else jnp.minimum(b + 1, blocks - 1)
                        keep(after, start(at, after, slots[after])[3])
                        low, ds = softmax(products)
                        gain[pending[1]] = gain[pending[1]] + complete(*pending)
                        pending = (b, h, low, ds)
                for s in range(slots[last_head]):
                    waiting[0, s] = pending[2][s]
                    waiting[1, s] = pending[3][s]
                return tuple(gain)

            keep(0, start(0, 0, slots[0])[3])
            waiting[...] = jnp.zeros_like(waiting)
            gain = list(
                lax.fori_loop(
                    0, blocks // UNROLL, step, (jnp.zeros((1, width), jnp.float32),) * heads
                )
            )
            gain[last_head] = gain[last_head] + complete(
                blocks - 1,
                last_head,
                [waiting[0, s] for s in range(slots[last_head])],
                [waiting[1, s] for s in range(slots[last_head])],
            )
            for h in range(heads):
                gains_ref[h : h + 1] = gain[h]

    extra = parts(jnp.concatenate([gains_ref[h : h + 1] for h in range(heads)], axis=1))
    names = [jnp.zeros((1, width), jnp.float32) + h.astype(jnp.float32) for h in owned]
    extra.append(jnp.concatenate(names, axis=1).astype(jnp.bfloat16))
    extra.append(jnp.zeros((SPARE - PARTS - 1, both), jnp.bfloat16))
    extra = jnp.concatenate(extra, axis=0)

    def finish(j, carry):
        for head in range(heads):
            out_ref[j, place(1, head)] = sums[head][j].astype(jnp.bfloat16)
        out_ref[j, span:] = extra
        return carry

    lax.fori_loop(0, blocks, finish, 0, unroll=4)


def attention(mine, table, lists, live, arrived, heads):
    blocks, span, both = arrived.shape
    vmem = pl.BlockSpec(memory_space=pltpu.VMEM)
    smem = pl.BlockSpec(memory_space=pltpu.SMEM)
    return pl.pallas_call(
        attention_kernel,
        in_specs=[smem, smem, smem, pl.BlockSpec(memory_space=pl.ANY), vmem],
        out_specs=vmem,
        out_shape=jax.ShapeDtypeStruct((blocks, span + SPARE, both), jnp.bfloat16),
        scratch_shapes=[pltpu.VMEM((blocks, both, BLK), jnp.bfloat16)] * heads
        + [pltpu.VMEM((blocks, BLK, both), jnp.float32)] * heads
        + [pltpu.VMEM((2, lists.shape[1], BLK, BLK), jnp.float32)] * heads
        + [pltpu.VMEM((heads, both // 2), jnp.float32)]
        + [pltpu.VMEM((2, lists.shape[1], BLK, BLK), jnp.bfloat16)]
        + [pltpu.SMEM(lists.shape, jnp.int32), pltpu.SemaphoreType.DMA(())],
        compiler_params=pltpu.CompilerParams(vmem_limit_bytes=24 << 20),
        name="attention",
    )(mine, table, live, lists, arrived)


def unpack_kernel(
    table_ref,
    back_ref,
    q_ref,
    k_ref,
    qg_ref,
    kg_ref,
    out_hbm,
    dq_hbm,
    dk_hbm,
    dv_hbm,
    done_ref,
    sems,
    copy_sems,
):
    groups, _, both = back_ref.shape
    width = both // 2
    tokens, features = q_ref.shape
    heads = features // (groups * width)
    step = tokens // CHUNKS
    moves, spots = [], []
    for head in range(groups * heads):
        group, slot = group_and_slot(table_ref[PLACE, head], groups)
        spots.append((group, slot))
        for n, hbm in enumerate((out_hbm, dv_hbm)):
            first = pl.multiple_of((n * heads + slot) * tokens, tokens)
            moves.append(
                pltpu.make_async_copy(
                    back_ref.at[group, pl.ds(first, tokens), pl.ds(width, width)],
                    hbm.at[:, pl.ds(head * width, width)],
                    copy_sems.at[head, n],
                )
            )
    for move in moves:
        move.start()
    for c in range(CHUNKS):
        for n, (raw_ref, gain_ref, hbm) in enumerate(
            ((q_ref, qg_ref, dq_hbm), (k_ref, kg_ref, dk_hbm))
        ):

            def some_rows(i, carry):
                row = pl.multiple_of(c * step + i * ROWS, ROWS)
                x = raw_ref[pl.ds(row, ROWS)].astype(jnp.float32)
                inverse = inverse_rms(x)
                unit = x * inverse
                pieces = []
                for group, slot in spots:
                    first = pl.multiple_of((n * heads + slot) * tokens + row, ROWS)
                    pieces.append(back_ref[group, pl.ds(first, ROWS), :width])
                grads = jnp.concatenate(pieces, axis=-1)
                g = grads.astype(jnp.float32) * gain_ref[...]
                mean = jnp.mean(g * unit, axis=-1, keepdims=True)
                done_ref[n, pl.ds(row, ROWS)] = (inverse * (g - unit * mean)).astype(jnp.bfloat16)
                return carry

            lax.fori_loop(0, step // ROWS, some_rows, 0)
            move = pltpu.make_async_copy(
                done_ref.at[n, pl.ds(c * step, step)], hbm.at[pl.ds(c * step, step)], sems.at[n, c]
            )
            move.start()
            moves.append(move)
    for move in moves:
        move.wait()


def unpack(table, back, q, k, q_gain, k_gain):
    groups, _, both = back.shape
    tokens, features = q.shape
    hbm = pl.BlockSpec(memory_space=pltpu.HBM)
    vmem = pl.BlockSpec(memory_space=pltpu.VMEM)
    return pl.pallas_call(
        unpack_kernel,
        in_specs=[pl.BlockSpec(memory_space=pltpu.SMEM)] + [vmem] * 5,
        out_specs=[hbm] * 4,
        out_shape=[jax.ShapeDtypeStruct((tokens, features), jnp.bfloat16)] * 4,
        scratch_shapes=[
            pltpu.VMEM((2, tokens, features), jnp.bfloat16),
            pltpu.SemaphoreType.DMA((2, CHUNKS)),
            pltpu.SemaphoreType.DMA((2 * features // both, 2)),
        ],
        compiler_params=pltpu.CompilerParams(vmem_limit_bytes=12 << 20),
        name="unpack",
    )(table, back, q, k, q_gain[None], k_gain[None])


def gains_kernel(back_ref, out_ref):
    groups, rows, both = back_ref.shape
    heads, width = out_ref.shape
    order = lax.broadcasted_iota(jnp.int32, (heads, width), 0).astype(jnp.float32)
    whole = jnp.zeros((heads, width), jnp.float32)
    for group in range(groups):
        extra = back_ref[group, rows - SPARE :].astype(jnp.float32)
        total = extra[0:1]
        for n in range(1, PARTS):
            total = total + extra[n : n + 1]
        names = extra[PARTS : PARTS + 1]
        for at in range(0, both, width):
            mine = order == names[:, at : at + width]
            whole = jnp.where(mine, total[:, at : at + width], whole)
    out_ref[...] = whole


def add_kernel(a_ref, b_ref, out_ref):
    out_ref[...] = a_ref[...] + b_ref[...]


def last_kernel(a_ref, b_ref, c_ref, d_ref, qg_ref, kg_ref, q_ref, k_ref):
    total = (a_ref[...] + b_ref[...]) + (c_ref[...] + d_ref[...])
    q_ref[...] = total / qg_ref[...]
    k_ref[...] = total / kg_ref[...]


def small_call(kernel, shapes, name, *args):
    return pl.pallas_call(
        kernel,
        in_specs=[pl.BlockSpec(memory_space=pltpu.VMEM)] * len(args),
        out_specs=[pl.BlockSpec(memory_space=pltpu.VMEM)] * len(shapes),
        out_shape=[jax.ShapeDtypeStruct(shape, jnp.float32) for shape in shapes],
        compiler_params=pltpu.CompilerParams(vmem_limit_bytes=2 << 20),
        name=name,
    )(*args)


def clip_gains(back, q_gain, k_gain):
    size = lax.axis_size("clip")
    rows = q_gain.shape[0] // BLK
    (one,) = small_call(gains_kernel, [(rows, BLK)], "gains", back)
    other = lax.ppermute(one, "clip", [(i, i ^ 1) for i in range(size)])
    (two,) = small_call(add_kernel, [(rows, BLK)], "add", one, other)
    terms = [
        lax.ppermute(two, "clip", [(i, (i + hop) % size) for i in range(size)]) for hop in (4, 2, 6)
    ]
    q, k = small_call(
        last_kernel,
        [(rows, BLK)] * 2,
        "last",
        two,
        *terms,
        q_gain.reshape(rows, BLK),
        k_gain.reshape(rows, BLK),
    )
    return q.reshape(-1), k.reshape(-1)


def shards(query_raw, key_raw, value, upstream, query_gain, key_gain, key_blocks, live):
    groups = lax.axis_size("seq")
    heads = key_blocks.shape[1] // groups
    mine = lax.axis_index("seq").reshape(1)
    lists = jnp.transpose(key_blocks[0], (1, 2, 0))
    packed, table = pack(
        live, query_raw[0], key_raw[0], value[0], upstream[0], query_gain, key_gain, groups, heads
    )
    packed, mine = lax.optimization_barrier((packed, mine))
    arrived = lax.all_to_all(packed, "seq", split_axis=0, concat_axis=0, tiled=True)
    results = attention(mine, table, lists, live, arrived, heads)
    back = lax.all_to_all(results, "seq", split_axis=0, concat_axis=0, tiled=True)
    attended, grad_query, grad_key, grad_value = unpack(
        table, back, query_raw[0], key_raw[0], query_gain, key_gain
    )
    q_total, k_total = clip_gains(back, query_gain, key_gain)
    return (
        attended[None],
        grad_query[None],
        grad_key[None],
        grad_value[None],
        q_total,
        k_total,
    )


def solution(mesh):
    tokens = P("clip", "seq", None)
    return jax.shard_map(
        shards,
        mesh=mesh,
        in_specs=(tokens,) * 4 + (P(), P(), P("clip", None, None, None), P("clip", None)),
        out_specs=(tokens,) * 4 + (P(), P()),
        check_vma=False,
    )
```

```python
import jax
import jax.numpy as jnp
from jax import lax
from jax.experimental import pallas as pl
from jax.experimental.pallas import tpu as pltpu
from jax.sharding import PartitionSpec as P

BLK = 128
EPSILON = 1e-06
ROWS = 64
CHUNKS = 2
PARTS = 3
SPARE = 8
UNROLL = 4
PLACE, ORDER = range(2)
QUERY, COTANGENT, KEY, VALUE = range(4)
GRAD_Q, OUT, GRAD_K, GRAD_V = range(4)
LOG2E = 1.4426950408889634


def contract(a, b, dims):
    return lax.dot_general(a, b, (dims, ((), ())), preferred_element_type=jnp.float32)


def inverse_rms(x):
    return lax.rsqrt(jnp.mean(x * x, axis=-1, keepdims=True) + EPSILON)


def rank_heads(live_ref, table_ref):
    count = table_ref.shape[1]
    lives = [live_ref[0, h] for h in range(count)]
    fours = [(n >= 4).astype(jnp.int32) for n in lives]
    somes = [(n >= 3).astype(jnp.int32) for n in lives]
    four, three, two = jnp.int32(0), sum(fours), sum(somes)
    for h in range(count):
        rank = jnp.where(fours[h] == 1, four, jnp.where(somes[h] == 1, three, two))
        table_ref[PLACE, h] = rank
        table_ref[ORDER, rank] = h
        four = four + fours[h]
        three = three + somes[h] - fours[h]
        two = two + 1 - somes[h]


def group_and_slot(rank, groups):
    second = rank >= groups
    return jnp.where(second, 2 * groups - 1 - rank, rank), second.astype(jnp.int32)


def pack_kernel(
    live_hbm,
    q_hbm,
    k_hbm,
    v_hbm,
    u_hbm,
    qg_hbm,
    kg_hbm,
    out_ref,
    table_ref,
    raw_ref,
    gain_ref,
    live_ref,
    raw_sems,
    gain_sems,
    copy_sems,
    live_sem,
):
    groups, span, both = out_ref.shape
    width = both // 2
    tokens = raw_ref.shape[1]
    heads = span // (2 * tokens)
    step = tokens // CHUNKS

    loads = [
        [
            pltpu.make_async_copy(
                hbm.at[pl.ds(c * step, step)],
                raw_ref.at[n, pl.ds(c * step, step)],
                raw_sems.at[n, c],
            )
            for c in range(CHUNKS)
        ]
        for n, hbm in enumerate((q_hbm, k_hbm))
    ]
    gain_loads = [
        pltpu.make_async_copy(hbm, gain_ref.at[n], gain_sems.at[n])
        for n, hbm in enumerate((qg_hbm, kg_hbm))
    ]
    live_load = pltpu.make_async_copy(live_hbm, live_ref, live_sem)
    live_load.start()
    for n in range(2):
        gain_loads[n].start()
        loads[n][0].start()
    for c in range(1, CHUNKS):
        for n in range(2):
            loads[n][c].start()
    live_load.wait()
    rank_heads(live_ref, table_ref)
    moves, spots = [], []
    for head in range(groups * heads):
        group, slot = group_and_slot(table_ref[PLACE, head], groups)
        spots.append((group, slot))
        for n, (hbm, pair) in enumerate(((u_hbm, 0), (v_hbm, 1))):
            first = pl.multiple_of((pair * heads + slot) * tokens, tokens)
            moves.append(
                pltpu.make_async_copy(
                    hbm.at[:, pl.ds(head * width, width)],
                    out_ref.at[group, pl.ds(first, tokens), pl.ds(width, width)],
                    copy_sems.at[head, n],
                )
            )
    for move in moves:
        move.start()
    for c in range(CHUNKS):
        for n in range(2):
            if c == 0:
                gain_loads[n].wait()
            loads[n][c].wait()

            def some_rows(i, carry):
                row = pl.multiple_of(c * step + i * ROWS, ROWS)
                x = raw_ref[n, pl.ds(row, ROWS)].astype(jnp.float32)
                y = (x * inverse_rms(x) * gain_ref[n]).astype(jnp.bfloat16)
                for head, (group, slot) in enumerate(spots):
                    first = pl.multiple_of((n * heads + slot) * tokens + row, ROWS)
                    at = head * width
                    out_ref[group, pl.ds(first, ROWS), :width] = y[:, at : at + width]
                return carry

            lax.fori_loop(0, step // ROWS, some_rows, 0)
    for move in moves:
        move.wait()


def in_hbm(x):
    return pltpu.with_memory_space_constraint(x, pltpu.HBM)


def pack(live, q, k, v, u, q_gain, k_gain, groups, heads):
    tokens, features = q.shape
    width = features // (groups * heads)
    hbm = pl.BlockSpec(memory_space=pltpu.HBM)
    vmem = pl.BlockSpec(memory_space=pltpu.VMEM)
    return pl.pallas_call(
        pack_kernel,
        in_specs=[hbm] * 7,
        out_specs=[vmem, pl.BlockSpec(memory_space=pltpu.SMEM)],
        out_shape=[
            jax.ShapeDtypeStruct((groups, 2 * heads * tokens, 2 * width), jnp.bfloat16),
            jax.ShapeDtypeStruct((2, groups * heads), jnp.int32),
        ],
        scratch_shapes=[
            pltpu.VMEM((2, tokens, features), jnp.bfloat16),
            pltpu.VMEM((2, 1, features), jnp.float32),
            pltpu.SMEM(live.shape, jnp.int32),
            pltpu.SemaphoreType.DMA((2, CHUNKS)),
            pltpu.SemaphoreType.DMA((2,)),
            pltpu.SemaphoreType.DMA((groups * heads, 2)),
            pltpu.SemaphoreType.DMA(()),
        ],
        compiler_params=pltpu.CompilerParams(vmem_limit_bytes=12 << 20),
        name="pack",
    )(*(in_hbm(x) for x in (live, q, k, v, u, q_gain[None], k_gain[None])))


def attention_kernel(mine_ref, table_ref, live_ref, lists_any, in_ref, out_ref, *scratch):
    *scratch, waiting, lists_ref, lists_sem = scratch
    lists_load = pltpu.make_async_copy(lists_any, lists_ref, lists_sem)
    lists_load.start()
    blocks, span, both = in_ref.shape
    heads = len(scratch) // 3
    width = both // 2
    scale = width ** (-0.5)
    turned, sums, ahead, gains_ref = scratch[:heads], scratch[heads : 2 * heads], scratch[2 * heads : -1], scratch[-1]
    mine = mine_ref[0]
    owned = [table_ref[ORDER, rank] for rank in (mine, 2 * blocks - 1 - mine)]
    live = [live_ref[0, h] for h in owned]

    def place(pair, head):
        return pl.ds((pair * heads + head) * BLK, BLK)

    def parts(row):
        pieces = []
        for _ in range(PARTS):
            pieces.append(row.astype(jnp.bfloat16))
            row = row - pieces[-1].astype(jnp.float32)
        return pieces

    def prepare(j, carry):
        for head in range(heads):
            turned[head][j] = in_ref[j, place(1, head)].T
            sums[head][j] = jnp.zeros((BLK, both), jnp.float32)
        return carry

    lax.fori_loop(0, blocks, prepare, 0, unroll=4)
    lists_load.wait()

    def start(b, head, slots):
        q = in_ref[b, place(0, head), :width]
        u = in_ref[b, place(0, head), width:]
        diagonal = (q, u)
        chosen = [lists_ref[b, s, owned[head]] for s in range(slots)]
        rows = jnp.concatenate([in_ref[j, place(1, head)] for j in chosen], axis=0)
        scores = contract(rows[:, :width], q, ((1,), (1,)))
        grads = contract(rows[:, width:], u, ((1,), (1,)))
        products = ([scores[s * BLK : (s + 1) * BLK] for s in range(slots)], [grads[s * BLK : (s + 1) * BLK] for s in range(slots)])
        return q, diagonal, chosen, products

    def softmax(products):
        scores, grads = products
        factor = scale * LOG2E
        tops = [jnp.max(s, axis=0, keepdims=True) * factor for s in scores]
        top = tops[0]
        for t in tops[1:]:
            top = jnp.maximum(top, t)
        raised = [jnp.exp2(s * factor - top) for s in scores]
        total = raised[0]
        inner = raised[0] * grads[0]
        for e, g in zip(raised[1:], grads[1:]):
            total = total + e
            inner = inner + e * g
        inverse = 1.0 / jnp.sum(total, axis=0, keepdims=True)
        delta = jnp.sum(inner, axis=0, keepdims=True) * inverse
        probs = [e * inverse for e in raised]
        low = [p.astype(jnp.bfloat16) for p in probs]
        ds = [(p * ((g - delta) * scale)).astype(jnp.bfloat16) for p, g in zip(probs, grads)]
        return low, ds

    def finish_block(b, head, q, diagonal, chosen, low, ds):
        keys = jnp.concatenate([turned[head][j, :width] for j in chosen], axis=1)
        values = jnp.concatenate([turned[head][j, width:] for j in chosen], axis=1)
        out_t = contract(values, jnp.concatenate(low, axis=0), ((1,), (0,)))
        dq_t = contract(keys, jnp.concatenate(ds, axis=0), ((1,), (0,)))
        q, u = diagonal
        more_k = contract(jnp.concatenate(ds, axis=0), q, ((1,), (0,)))
        more_v = contract(jnp.concatenate(low, axis=0), u, ((1,), (0,)))
        old = [sums[head][j] for j in chosen]
        for s, (j, o) in enumerate(zip(chosen, old)):
            sums[head][j, :, :width] = o[:, :width] + more_k[s * BLK : (s + 1) * BLK]
            sums[head][j, :, width:] = o[:, width:] + more_v[s * BLK : (s + 1) * BLK]
        dq = dq_t.astype(jnp.bfloat16).T
        out_ref[b, place(0, head), :width] = dq
        out_ref[b, place(0, head), width:] = out_t.astype(jnp.bfloat16).T
        return jnp.sum(dq.astype(jnp.float32) * q.astype(jnp.float32), axis=0, keepdims=True)

    for slots in ((2, 2), (3, 2), (3, 3), (4, 2), (4, 3), (4, 4)):

        @pl.when(jnp.logical_and(live[0] == slots[0], live[1] == slots[1]))
        def _():
            def keep(h, products):
                for s in range(slots[h]):
                    for n in range(2):
                        ahead[h][n, s] = products[n][s]

            last_head = heads - 1

            def complete(b, h, low, ds):
                rows = in_ref[b, place(0, h)]
                q, u = rows[:, :width], rows[:, width:]
                chosen = [lists_ref[b, s, owned[h]] for s in range(slots[h])]
                return finish_block(b, h, q, (q, u), chosen, low, ds)

            def step(i, gain):
                gain = list(gain)
                before = jnp.maximum(UNROLL * i - 1, 0)
                pending = (
                    before,
                    last_head,
                    [waiting[0, s] for s in range(slots[last_head])],
                    [waiting[1, s] for s in range(slots[last_head])],
                )
                for k in range(UNROLL):
                    b = UNROLL * i + k
                    for h in range(heads):
                        products = [[ahead[h][n, s] for s in range(slots[h])] for n in range(2)]
                        after = h + 1 if h + 1 < heads else 0
                        at = b if h + 1 < heads else jnp.minimum(b + 1, blocks - 1)
                        keep(after, start(at, after, slots[after])[3])
                        low, ds = softmax(products)
                        gain[pending[1]] = gain[pending[1]] + complete(*pending)
                        pending = (b, h, low, ds)
                for s in range(slots[last_head]):
                    waiting[0, s] = pending[2][s]
                    waiting[1, s] = pending[3][s]
                return tuple(gain)

            keep(0, start(0, 0, slots[0])[3])
            waiting[...] = jnp.zeros_like(waiting)
            gain = list(
                lax.fori_loop(
                    0, blocks // UNROLL, step, (jnp.zeros((1, width), jnp.float32),) * heads
                )
            )
            gain[last_head] = gain[last_head] + complete(
                blocks - 1,
                last_head,
                [waiting[0, s] for s in range(slots[last_head])],
                [waiting[1, s] for s in range(slots[last_head])],
            )
            for h in range(heads):
                gains_ref[h : h + 1] = gain[h]

    extra = parts(jnp.concatenate([gains_ref[h : h + 1] for h in range(heads)], axis=1))
    names = [jnp.zeros((1, width), jnp.float32) + h.astype(jnp.float32) for h in owned]
    extra.append(jnp.concatenate(names, axis=1).astype(jnp.bfloat16))
    extra.append(jnp.zeros((SPARE - PARTS - 1, both), jnp.bfloat16))
    extra = jnp.concatenate(extra, axis=0)

    def finish(j, carry):
        for head in range(heads):
            out_ref[j, place(1, head)] = sums[head][j].astype(jnp.bfloat16)
        out_ref[j, span:] = extra
        return carry

    lax.fori_loop(0, blocks, finish, 0, unroll=4)


def attention(mine, table, lists, live, arrived, heads):
    blocks, span, both = arrived.shape
    vmem = pl.BlockSpec(memory_space=pltpu.VMEM)
    smem = pl.BlockSpec(memory_space=pltpu.SMEM)
    return pl.pallas_call(
        attention_kernel,
        in_specs=[smem, smem, smem, pl.BlockSpec(memory_space=pl.ANY), vmem],
        out_specs=vmem,
        out_shape=jax.ShapeDtypeStruct((blocks, span + SPARE, both), jnp.bfloat16),
        scratch_shapes=[pltpu.VMEM((blocks, both, BLK), jnp.bfloat16)] * heads
        + [pltpu.VMEM((blocks, BLK, both), jnp.float32)] * heads
        + [pltpu.VMEM((2, lists.shape[1], BLK, BLK), jnp.float32)] * heads
        + [pltpu.VMEM((heads, both // 2), jnp.float32)]
        + [pltpu.VMEM((2, lists.shape[1], BLK, BLK), jnp.bfloat16)]
        + [pltpu.SMEM(lists.shape, jnp.int32), pltpu.SemaphoreType.DMA(())],
        compiler_params=pltpu.CompilerParams(vmem_limit_bytes=24 << 20),
        name="attention",
    )(mine, table, live, lists, arrived)


def unpack_kernel(
    table_ref,
    back_ref,
    q_ref,
    k_ref,
    qg_ref,
    kg_ref,
    out_hbm,
    dq_hbm,
    dk_hbm,
    dv_hbm,
    done_ref,
    sems,
    copy_sems,
):
    groups, _, both = back_ref.shape
    width = both // 2
    tokens, features = q_ref.shape
    heads = features // (groups * width)
    step = tokens // CHUNKS
    moves, spots = [], []
    for head in range(groups * heads):
        group, slot = group_and_slot(table_ref[PLACE, head], groups)
        spots.append((group, slot))
        for n, hbm in enumerate((out_hbm, dv_hbm)):
            first = pl.multiple_of((n * heads + slot) * tokens, tokens)
            moves.append(
                pltpu.make_async_copy(
                    back_ref.at[group, pl.ds(first, tokens), pl.ds(width, width)],
                    hbm.at[:, pl.ds(head * width, width)],
                    copy_sems.at[head, n],
                )
            )
    for move in moves:
        move.start()
    for c in range(CHUNKS):
        for n, (raw_ref, gain_ref, hbm) in enumerate(
            ((q_ref, qg_ref, dq_hbm), (k_ref, kg_ref, dk_hbm))
        ):

            def some_rows(i, carry):
                row = pl.multiple_of(c * step + i * ROWS, ROWS)
                x = raw_ref[pl.ds(row, ROWS)].astype(jnp.float32)
                inverse = inverse_rms(x)
                unit = x * inverse
                pieces = []
                for group, slot in spots:
                    first = pl.multiple_of((n * heads + slot) * tokens + row, ROWS)
                    pieces.append(back_ref[group, pl.ds(first, ROWS), :width])
                grads = jnp.concatenate(pieces, axis=-1)
                g = grads.astype(jnp.float32) * gain_ref[...]
                mean = jnp.mean(g * unit, axis=-1, keepdims=True)
                done_ref[n, pl.ds(row, ROWS)] = (inverse * (g - unit * mean)).astype(jnp.bfloat16)
                return carry

            lax.fori_loop(0, step // ROWS, some_rows, 0)
            move = pltpu.make_async_copy(
                done_ref.at[n, pl.ds(c * step, step)], hbm.at[pl.ds(c * step, step)], sems.at[n, c]
            )
            move.start()
            moves.append(move)
    for move in moves:
        move.wait()


def unpack(table, back, q, k, q_gain, k_gain):
    groups, _, both = back.shape
    tokens, features = q.shape
    hbm = pl.BlockSpec(memory_space=pltpu.HBM)
    vmem = pl.BlockSpec(memory_space=pltpu.VMEM)
    return pl.pallas_call(
        unpack_kernel,
        in_specs=[pl.BlockSpec(memory_space=pltpu.SMEM)] + [vmem] * 5,
        out_specs=[hbm] * 4,
        out_shape=[jax.ShapeDtypeStruct((tokens, features), jnp.bfloat16)] * 4,
        scratch_shapes=[
            pltpu.VMEM((2, tokens, features), jnp.bfloat16),
            pltpu.SemaphoreType.DMA((2, CHUNKS)),
            pltpu.SemaphoreType.DMA((2 * features // both, 2)),
        ],
        compiler_params=pltpu.CompilerParams(vmem_limit_bytes=12 << 20),
        name="unpack",
    )(table, back, q, k, q_gain[None], k_gain[None])


def gains_kernel(back_ref, out_ref):
    groups, rows, both = back_ref.shape
    heads, width = out_ref.shape
    order = lax.broadcasted_iota(jnp.int32, (heads, width), 0).astype(jnp.float32)
    whole = jnp.zeros((heads, width), jnp.float32)
    for group in range(groups):
        extra = back_ref[group, rows - SPARE :].astype(jnp.float32)
        total = extra[0:1]
        for n in range(1, PARTS):
            total = total + extra[n : n + 1]
        names = extra[PARTS : PARTS + 1]
        for at in range(0, both, width):
            mine = order == names[:, at : at + width]
            whole = jnp.where(mine, total[:, at : at + width], whole)
    out_ref[...] = whole


def add_kernel(a_ref, b_ref, out_ref):
    out_ref[...] = a_ref[...] + b_ref[...]


def last_kernel(a_ref, b_ref, c_ref, d_ref, qg_ref, kg_ref, q_ref, k_ref):
    total = (a_ref[...] + d_ref[...]) + (b_ref[...] + c_ref[...])
    q_ref[...] = total / qg_ref[...]
    k_ref[...] = total / kg_ref[...]


def small_call(kernel, shapes, name, *args):
    return pl.pallas_call(
        kernel,
        in_specs=[pl.BlockSpec(memory_space=pltpu.VMEM)] * len(args),
        out_specs=[pl.BlockSpec(memory_space=pltpu.VMEM)] * len(shapes),
        out_shape=[jax.ShapeDtypeStruct(shape, jnp.float32) for shape in shapes],
        compiler_params=pltpu.CompilerParams(vmem_limit_bytes=2 << 20),
        name=name,
    )(*args)


def clip_gains(back, q_gain, k_gain):
    size = lax.axis_size("clip")
    rows = q_gain.shape[0] // BLK
    (one,) = small_call(gains_kernel, [(rows, BLK)], "gains", back)
    other = lax.ppermute(one, "clip", [(i, i ^ 1) for i in range(size)])
    (two,) = small_call(add_kernel, [(rows, BLK)], "add", one, other)
    terms = [
        lax.ppermute(two, "clip", [(i, (i + hop) % size) for i in range(size)]) for hop in (6, 2, 4)
    ]
    q, k = small_call(
        last_kernel,
        [(rows, BLK)] * 2,
        "last",
        two,
        *terms,
        q_gain.reshape(rows, BLK),
        k_gain.reshape(rows, BLK),
    )
    return q.reshape(-1), k.reshape(-1)


def shards(query_raw, key_raw, value, upstream, query_gain, key_gain, key_blocks, live):
    groups = lax.axis_size("seq")
    heads = key_blocks.shape[1] // groups
    mine = lax.axis_index("seq").reshape(1)
    lists = jnp.transpose(key_blocks[0], (1, 2, 0))
    packed, table = pack(
        live, query_raw[0], key_raw[0], value[0], upstream[0], query_gain, key_gain, groups, heads
    )
    packed, mine = lax.optimization_barrier((packed, mine))
    arrived = lax.all_to_all(packed, "seq", split_axis=0, concat_axis=0, tiled=True)
    results = attention(mine, table, lists, live, arrived, heads)
    back = lax.all_to_all(results, "seq", split_axis=0, concat_axis=0, tiled=True)
    attended, grad_query, grad_key, grad_value = unpack(
        table, back, query_raw[0], key_raw[0], query_gain, key_gain
    )
    q_total, k_total = clip_gains(back, query_gain, key_gain)
    return (
        attended[None],
        grad_query[None],
        grad_key[None],
        grad_value[None],
        q_total,
        k_total,
    )


def solution(mesh):
    tokens = P("clip", "seq", None)
    return jax.shard_map(
        shards,
        mesh=mesh,
        in_specs=(tokens,) * 4 + (P(), P(), P("clip", None, None, None), P("clip", None)),
        out_specs=(tokens,) * 4 + (P(), P()),
        check_vma=False,
    )
```
